128 devices in a mesh: row: 8 (over z, x_hi), col: 16 (over x_lo, y, core).
Axes of the slice: x: 4 (x_hi: 2, x_lo: 2; x = x_hi * 2 + x_lo), y: 4, z: 4, core: 2. Of those that a mesh axis runs over, the one named last changes fastest.
Arguments:
- factor: float32 [16384, 16384], P(('row', 'col')), as said below
- damping: float32 [16384], P(('row', 'col')), may hold values from 0.1 to 1
- gradients: float32 [3072, 128], replicated, may hold values from -6 to 6
- inverses: float32 [5, 512, 512], replicated, as said below
Outputs:
- updated: float32 [8, 8, 256, 4, 16, 256], P(None, 'row', None, None, 'col')
- panel_tiles: float32 [8, 8, 256, 512], P(None, 'row', 'col')
- solution: float32 [3072, 128], replicated
The draws below stay inside these ranges and needn't reach their ends.
Inputs may be any that keep to these rules, and one draw needn't show every extreme that they name: `factor`: symmetric. `inverses`: one matrix for each diagonal block after the first.
All inputs are finite; a program needn't handle non-finite values.
Results may differ from the reference program's by a relative error of at most 0.0001.
Values sent between devices are 32-bit elements; how exact they have to be, the bound alone decides.
No kernel may reach another device: no remote copies, remote signals or barrier semaphores. Data moves between devices by JAX's collectives and lax.ppermute only.
A program may use at most 128 MiB of HBM per device.

```python
import math
import jax
import jax.numpy as jnp
from jax import lax

ORDER = 16384
PANEL = 512
GRADS = 128
BLOCKS = 6
TILE = 256
SOLVED = 3072
N_ROW = 8
N_COL = 16


def draw_factor(key, part):
    first_key, second_key = jax.random.split(jax.random.fold_in(key, 11))
    uniform_part = jax.random.uniform(first_key, (ORDER, ORDER), jnp.float32, -1.0, 1.0)
    index_line = jnp.arange(ORDER)
    upper_mask = index_line[:, None] < index_line[None, :]
    symmetric = jnp.where(upper_mask, uniform_part, uniform_part.T)
    diagonal_part = jax.random.uniform(second_key, (ORDER,), jnp.float32, 1.0, 2.0)
    scale_off = 0.7 / math.sqrt(ORDER)
    off_part = symmetric * scale_off
    return jnp.where(index_line[:, None] == index_line[None, :], diagonal_part[:, None], off_part)


def draw_inverses(key, part):
    first_key, second_key = jax.random.split(jax.random.fold_in(key, 23))
    off_part = 0.01 * jax.random.normal(first_key, (BLOCKS - 1, PANEL, PANEL), jnp.float32)
    diagonal_part = jax.random.uniform(second_key, (BLOCKS - 1, PANEL, 1), jnp.float32, 0.4, 0.9)
    index_line = jnp.arange(PANEL)
    on_diagonal = index_line[:, None] == index_line[None, :]
    return jnp.where(on_diagonal[None], diagonal_part, off_part)


def shard_levels(key, dims, cuts, least, largest):
    loudness = 1.0
    for position, shards_of in cuts:
        draws = jax.random.uniform(jax.random.fold_in(jax.random.fold_in(key, 6), position), (shards_of,), jnp.float32, least / len(cuts), largest / len(cuts))
        loudness = loudness * jnp.repeat(jnp.exp(draws), dims[position] // shards_of).reshape((-1,) + (1,) * (len(dims) - 1 - position))
    return loudness


def normal_values(stream_key, dims, scale, limit, dtype=jnp.bfloat16):
    return jnp.clip(scale * jax.random.normal(stream_key, dims, jnp.float32), -limit, limit).astype(dtype)


def setup_inputs(seed: int = 0) -> dict:
    arg_keys = jax.random.split(jax.random.key(seed), 5)
    factor = draw_factor(jax.random.fold_in(arg_keys[4], 71), 0)
    damping = jnp.clip(jnp.exp(math.log(1.0) - 2.3025851 * jax.random.uniform(arg_keys[1], (ORDER,), jnp.float32) ** shard_levels(arg_keys[1], (ORDER,), ((0, 128),), -0.2, 0.2)), 0.1, 1.0)
    gradients = normal_values(arg_keys[2], (SOLVED, GRADS), 1.0, 6.0, jnp.float32)
    inverses = draw_inverses(jax.random.fold_in(arg_keys[4], 71), 0)
    return dict(factor=factor, damping=damping, gradients=gradients, inverses=inverses)


def right_solve(corner_factor, panel_rows):
    return jax.scipy.linalg.solve_triangular(corner_factor, panel_rows.T, lower=True).T

def exact_dot(left, right):
    return jnp.dot(left.astype(jnp.float32), right.astype(jnp.float32), precision=lax.Precision.HIGHEST, preferred_element_type=jnp.float32)

def reference(factor, damping, gradients, inverses):
    diagonal_index = jnp.arange(ORDER)
    damped = factor.at[diagonal_index, diagonal_index].add(damping)
    corner_factor = jnp.linalg.cholesky(damped[:PANEL, :PANEL])
    panel_factor = right_solve(corner_factor, damped[:, :PANEL])
    row_blocks = damped.reshape(ORDER // PANEL, PANEL, ORDER)
    lead_blocks = panel_factor.reshape(ORDER // PANEL, PANEL, PANEL)

    def update_block(row_pair):
        block_rows, lead_rows = row_pair
        product = lax.dot_general(lead_rows.astype(jnp.float32), panel_factor.astype(jnp.float32), (((1,), (1,)), ((), ())), precision=lax.Precision.HIGHEST, preferred_element_type=jnp.float32)
        return block_rows - product
    schur = lax.map(update_block, (row_blocks, lead_blocks)).reshape(ORDER, ORDER)
    first_block = jax.scipy.linalg.solve_triangular(corner_factor, gradients[:PANEL], lower=True)
    solved = [first_block]
    for block_index in range(1, BLOCKS):
        low = block_index * PANEL
        high = low + PANEL
        known = exact_dot(panel_factor[low:high], first_block)
        if block_index > 1:
            earlier = jnp.concatenate(solved[1:], axis=0)
            known = known + exact_dot(schur[low:high, PANEL:low], earlier)
        solved.append(exact_dot(inverses[block_index - 1], gradients[low:high] - known))
    solution = jnp.concatenate(solved, axis=0)
    updated = schur.reshape(N_ROW, N_ROW, TILE, N_ROW * N_ROW // N_COL, N_COL, TILE)
    panel_tiles = panel_factor.reshape(N_ROW, N_ROW, TILE, PANEL)
    return (updated, panel_tiles, solution)
```

```python
import functools

import jax
import jax.numpy as jnp
from jax import lax
from jax.experimental import pallas as pl
from jax.experimental.pallas import tpu as pltpu
from jax.sharding import Mesh
from jax.sharding import PartitionSpec as P


INTERPRET = False
CHUNKS = 2
FIRST_STEPS = 1
ALL = ("z", "xh", "xl", "y", "core")
VMEM = pl.BlockSpec(memory_space=pltpu.VMEM)
SMEM = pl.BlockSpec(memory_space=pltpu.SMEM)
ANY = pl.BlockSpec(memory_space=pl.ANY)
F32 = jnp.float32


def shape(*dims):
    return jax.ShapeDtypeStruct(dims, F32)


def dot(left, right, dims):
    return lax.dot_general(
        left, right, (dims, ((), ())), precision=lax.Precision.HIGHEST, preferred_element_type=F32
    )


def halves(value):
    high = value.astype(jnp.bfloat16)
    return high, (value - high.astype(F32)).astype(jnp.bfloat16)


def dot3(left, right, dims):
    one = lambda a, b: lax.dot_general(a, b, (dims, ((), ())), preferred_element_type=F32)
    return one(left[0], right[0]) + (one(left[0], right[1]) + one(left[1], right[0]))


NN = ((1,), (0,))
NT = ((1,), (1,))
TN = ((0,), (0,))


def device_of(z, xh, xl, y, core):
    return (((z * 2 + xh) * 2 + xl) * 4 + y) * 2 + core


def every():
    return [
        (z, xh, xl, y, core)
        for z in range(4)
        for xh in range(2)
        for xl in range(2)
        for y in range(4)
        for core in range(2)
    ]


def swap(value, dz=0, dx=0, dy=0, dcore=0, only=None):
    pairs = []
    for z, xh, xl, y, core in every():
        if only is None or only(z, xh * 2 + xl, y, core):
            to = (z ^ dz, xh ^ (dx >> 1), xl ^ (dx & 1), y ^ dy, core ^ dcore)
            pairs.append((device_of(z, xh, xl, y, core), device_of(*to)))
    return lax.ppermute(value, ALL, pairs)


def factor_block(block):
    size = block.shape[0]
    lane = lax.broadcasted_iota(jnp.int32, (8, size), 1)
    sub = lax.broadcasted_iota(jnp.int32, (8, size), 0)
    left = [block[8 * i : 8 * i + 8, :] for i in range(size // 8)]
    right = [jnp.where(lane == sub + 8 * i, 1.0, 0.0).astype(F32) for i in range(size // 8)]
    for k in range(size - 1):
        b, s = divmod(k, 8)
        inverse = 1.0 / left[b][s : s + 1, k : k + 1]
        left_row = jnp.broadcast_to(left[b][s : s + 1, :] * inverse, (8, size))
        right_row = jnp.broadcast_to(right[b][s : s + 1, :] * inverse, (8, size))
        for i in range(b if s < 7 else b + 1, size // 8):
            col = jnp.broadcast_to(left[i][:, k : k + 1], (8, size))
            if i == b:
                col = jnp.where(sub > s, col, 0.0)
            left[i] = left[i] - col * left_row
            right[i] = right[i] - col * right_row
    rows = []
    for i in range(size // 8):
        pivot = jnp.sum(jnp.where(lane == sub + 8 * i, left[i], 0.0), axis=1, keepdims=True)
        rows.append(right[i] * (1.0 / jnp.sqrt(pivot)))
    return jnp.concatenate(rows, axis=0)


def eliminate(w_ref, x_ref, low_step, high_step):
    n = x_ref.shape[0]
    nb = n // 4

    def step(j, carry):
        at = pl.multiple_of(j * nb, nb)
        xj = factor_block(w_ref[pl.ds(at, nb), pl.ds(at, nb)])
        low = dot(w_ref[:, pl.ds(at, nb)], xj, NT)
        rows = lax.broadcasted_iota(jnp.int32, (n, nb), 0)
        low = jnp.where(rows >= at + nb, low, 0.0)
        w_ref[...] = w_ref[...] - dot(low, low, NT)
        xr = dot(xj, x_ref[pl.ds(at, nb), :], NN)
        x_ref[pl.ds(at, nb), :] = xr
        x_ref[...] = x_ref[...] - dot(low, xr, NN)
        return carry

    lax.fori_loop(low_step, high_step, step, 0)


def corner_kernel(spot_ref, *refs):
    pieces = refs[:4]
    x_ref, w_ref = refs[-2:]
    n = x_ref.shape[0]
    part = pieces[0].shape[1]
    z = spot_ref[0]
    core = spot_ref[4]
    for q in range(4):
        for i in range(4):
            side = core if i < 2 else 1 - core
            row = pl.multiple_of((i % 2) * (n // 2) + side * (n // 4) + (z ^ q) * part, part)
            w_ref[pl.ds(row, part), :] = pieces[q][i]
    ri = lax.broadcasted_iota(jnp.int32, (n, n), 0)
    ci = lax.broadcasted_iota(jnp.int32, (n, n), 1)
    x_ref[...] = jnp.where(ri == ci, 1.0, 0.0).astype(F32)
    eliminate(w_ref, x_ref, 0, FIRST_STEPS)


def corner_end_kernel(x_in, w_in, x_ref, square_ref, w_ref):
    x_ref[...] = x_in[...]
    w_ref[...] = w_in[...]
    eliminate(w_ref, x_ref, FIRST_STEPS, 4)
    x = x_ref[...]
    square_ref[...] = dot(x, x, TN)


def inverse_factor(spot, pieces):
    n = pieces[0].shape[2]
    square = shape(n, n)
    state = pl.pallas_call(
        corner_kernel,
        out_shape=[square, square],
        in_specs=[SMEM] + [VMEM] * 4,
        out_specs=[VMEM, VMEM],
        interpret=INTERPRET,
        name="inverse_start",
    )(spot, *pieces)
    return pl.pallas_call(
        corner_end_kernel,
        out_shape=[square, square],
        in_specs=[VMEM, VMEM],
        out_specs=[VMEM, VMEM],
        scratch_shapes=[pltpu.VMEM((n, n), F32)],
        interpret=INTERPRET,
        name="inverse_end",
    )(*state)


def corner_lines(panel):
    source = lambda zz, xx, yy, cc: zz == 0 and xx == 0 and yy < 2
    return [swap(panel, dy=d, only=source) for d in (1, 2, 3)]


def corner_both(panel, got, y):
    upper = jnp.where(y == 0, panel, jnp.where(y == 1, got[0], jnp.where(y == 2, got[1], got[2])))
    lower = jnp.where(y == 1, panel, jnp.where(y == 0, got[0], jnp.where(y == 3, got[1], got[2])))
    return jnp.stack([upper, lower])


def spread_corner(own, other, z, x):
    whole = jnp.concatenate([own, other], axis=0)
    part = whole.shape[1] // 4
    pieces = [whole[:, d * part : (d + 1) * part] for d in range(4)]
    first = lambda zz, xx, yy, cc: zz == 0 and xx == 0
    got = [swap(pieces[d], dz=d, only=first) for d in (1, 2, 3)]
    value = jnp.where(z == 0, pieces[0], got[0] + got[1] + got[2])
    second = lambda zz, xx, yy, cc: xx == 0
    got = [swap(value, dx=d, only=second) for d in (1, 2, 3)]
    value = jnp.where(x == 0, value, got[0] + got[1] + got[2])
    return [value] + [swap(value, dz=d) for d in (1, 2, 3)]


def pack_first_kernel(spot_ref, factor_ref, damping_ref, out_ref, hold, *, chunk, width):
    rows = hold.shape[0]
    part = damping_ref.shape[1]
    z, xh, xl, y, core = (spot_ref[i] for i in range(5))
    hold[...] = factor_ref[...]
    device = (((z * 2 + xh) * 2 + xl) * 4 + y) * 2 + core
    at = pl.multiple_of(device * part, part)
    lane = lax.broadcasted_iota(jnp.int32, (rows, part), 1)
    sub = lax.broadcasted_iota(jnp.int32, (rows, part), 0)
    add = jnp.where(lane == sub + chunk * rows, jnp.broadcast_to(damping_ref[...], (rows, part)), 0.0)
    hold[:, pl.ds(at, part)] = hold[:, pl.ds(at, part)] + add
    for m in range(8):
        for side in range(2):
            for b in range(4):
                col = (b * 2 + side) * 8 + m
                out_ref[m, :, (side * 4 + b) * width : (side * 4 + b + 1) * width] = hold[
                    :, col * width : (col + 1) * width
                ]


def pack_first(spot, factor, damping, chunk):
    part, order = factor.shape
    rows = part // CHUNKS
    width = order // 64
    return pl.pallas_call(
        functools.partial(pack_first_kernel, chunk=chunk, width=width),
        out_shape=shape(8, rows, 8 * width),
        grid=(1,),
        in_specs=[SMEM, pl.BlockSpec((rows, order), lambda i: (chunk, 0)), VMEM],
        out_specs=VMEM,
        scratch_shapes=[pltpu.VMEM((rows, order), F32)],
        interpret=INTERPRET,
        name="pack_first",
    )(spot, factor, damping)


def pack_second_kernel(spot_ref, in_ref, *refs):
    outs = refs[-4:]
    rows = in_ref.shape[1]
    half = in_ref.shape[2] // 2
    xh, xl = spot_ref[1], spot_ref[2]
    for n in range(4):
        col = pl.multiple_of((xl ^ (n & 1)) * half, half)
        for y1 in range(2):
            for k in range(2):
                m = y1 * 4 + (xh ^ (n >> 1)) * 2 + k
                at = (y1 * 2 + k) * rows
                outs[n][at : at + rows, :] = in_ref[m, :, pl.ds(col, half)]


def pack_third_kernel(spot_ref, *refs):
    ins, outs = refs[:4], refs[-4:]
    half = ins[0].shape[0] // 2
    z, xl = spot_ref[0], spot_ref[2]
    flip = (xl ^ (z >> 1)) == 1
    for q in range(4):
        row = pl.multiple_of(((z & 1) ^ (q & 1)) * half, half)
        for n1 in range(2):
            same = ins[n1 * 2 + (q >> 1)][pl.ds(row, half), :]
            changed = ins[n1 * 2 + 1 - (q >> 1)][pl.ds(row, half), :]
            outs[q][n1 * half : (n1 + 1) * half, :] = jnp.where(flip, changed, same)


def repack(kernel, spot, arrays, out, after=()):
    return pl.pallas_call(
        kernel,
        out_shape=[out] * 4,
        in_specs=[SMEM] + [VMEM] * len(arrays) + [ANY] * len(after),
        out_specs=[VMEM] * 4,
        interpret=INTERPRET,
    )(spot, *arrays, *after)


def send_chunk(spot, factor, damping, chunk, after):
    first = pack_first(spot, factor, damping, chunk)
    first = lax.all_to_all(first, ("y", "core"), 0, 0, tiled=True)
    _, rows, cols = first.shape
    out = shape(4 * rows, cols // 2)
    second = repack(pack_second_kernel, spot, [first], out, after)
    second = [second[n] if n == 0 else swap(second[n], dx=n) for n in range(4)]
    third = repack(pack_third_kernel, spot, second, out)
    return [third[q] if q == 0 else swap(third[q], dz=q) for q in range(4)]


def panel_kernel(spot_ref, x_ref, rows_ref, cols_ref, row_ref, col_ref, tile_ref):
    part = rows_ref.shape[0] // 16
    xl, y, core = spot_ref[2], spot_ref[3], spot_ref[4]
    x = halves(x_ref[...])
    row_ref[...] = dot3(halves(rows_ref[...]), x, NT)
    col_ref[...] = dot3(halves(cols_ref[...]), x, NT)
    share = part // 8
    column = (xl * 4 + y) * 2 + core
    for a in range(8):
        at = pl.multiple_of(a * 2 * part + column * share, share)
        tile_ref[a * share : (a + 1) * share, :] = row_ref[pl.ds(at, share), :]


def panel_solve(spot, x, rows_in, cols_in):
    width = x.shape[0]
    return pl.pallas_call(
        panel_kernel,
        out_shape=[shape(*rows_in.shape), shape(*cols_in.shape), shape(rows_in.shape[0] // 16, width)],
        in_specs=[SMEM, VMEM, VMEM, VMEM],
        out_specs=[VMEM] * 3,
        interpret=INTERPRET,
        name="panel_solve",
    )(spot, x, rows_in, cols_in)


def share_rows(panel):
    pairs = []
    for z, xh, xl, y, core in every():
        to = (xl * 2 + (y >> 1), y & 1, z >> 1, (z & 1) * 2 + xh, core)
        pairs.append((device_of(z, xh, xl, y, core), device_of(*to)))
    return lax.ppermute(panel, ALL, pairs)


def share_cols(panel):
    pairs = []
    for z, xh, xl, y, core in every():
        to = (z, core, xh, xl * 2 + (y >> 1), y & 1)
        pairs.append((device_of(z, xh, xl, y, core), device_of(*to)))
    return lax.ppermute(panel, ALL, pairs)


def update_kernel(spot_ref, *refs):
    blocks = refs[:4]
    row_ref, col_ref = refs[4:6]
    out_ref, high_ref, low_ref, hold = refs[-4:]
    count, _, rows, width = row_ref.shape
    xh = spot_ref[1]
    step = pl.program_id(0)
    half = 2 * rows

    @pl.when(step == 0)
    def _():
        high_ref[...], low_ref[...] = halves(col_ref[...])

    for q in range(4):

        @pl.when(step == q)
        def _():
            for n in range(2):
                at = pl.multiple_of((xh ^ n) * half, half)
                hold[pl.ds(at, half), :] = blocks[q][n * half : (n + 1) * half, :]

    left = halves(row_ref[...].reshape(count * rows, width))
    hold[...] = hold[...] - dot3(left, (high_ref[...], low_ref[...]), NT)
    lanes = out_ref.shape[3]
    groups = hold.shape[1] // lanes
    for i in range(count):
        for g in range(groups):
            out_ref.at[i, 0][pl.ds(g, rows, stride=groups), :] = hold[
                i * rows : (i + 1) * rows, g * lanes : (g + 1) * lanes
            ]


def update(spot, blocks, row_factor, col_factor, out, chunk):
    height, local_cols = blocks[0].shape
    rows = height // 4
    width = row_factor.shape[1]
    lanes = local_cols // 8
    first = out is None
    full = lambda a: pl.BlockSpec(a.shape, lambda i, s: (0, 0))
    place = lambda i, s: (s[0] ^ i, chunk, 0, 0)
    operands = [*blocks, row_factor.reshape(16, CHUNKS, rows, width), col_factor]
    return pl.pallas_call(
        update_kernel,
        out_shape=shape(16, CHUNKS, rows * 8, lanes),
        grid_spec=pltpu.PrefetchScalarGridSpec(
            num_scalar_prefetch=1,
            grid=(4,),
            in_specs=[full(b) for b in blocks]
            + [pl.BlockSpec((4, 1, rows, width), place), full(col_factor)]
            + ([] if first else [ANY]),
            out_specs=pl.BlockSpec((4, 1, rows * 8, lanes), place),
            scratch_shapes=[
                pltpu.VMEM(col_factor.shape, jnp.bfloat16),
                pltpu.VMEM(col_factor.shape, jnp.bfloat16),
                pltpu.VMEM((height, local_cols), F32),
            ],
        ),
        input_output_aliases={} if first else {7: 0},
        interpret=INTERPRET,
        name="update",
    )(spot, *operands, *([] if first else [out]))


def on_line(z, x, y, core):
    return z == 0 and x == 2


def place_panels_kernel(spot_ref, own_ref, other_ref, out_ref):
    part = own_ref.shape[1] // 2
    y, core = spot_ref[3], spot_ref[4]
    for ref, side in ((own_ref, core), (other_ref, 1 - core)):
        for m in range(4):
            line = y ^ m
            for slot, tile in ((0, 4 + line), (1, line + 8 * (1 - line // 2))):
                at = (tile * 2 + side) * part
                out_ref[:, pl.ds(pl.multiple_of(at, part), part)] = ref[
                    m, slot * part : (slot + 1) * part, :
                ].T


def place_panels(spot, own, other):
    _, rows, width = own.shape
    return pl.pallas_call(
        place_panels_kernel,
        out_shape=shape(width, 12 * rows),
        in_specs=[SMEM, VMEM, VMEM],
        out_specs=VMEM,
        interpret=INTERPRET,
        name="place_panels",
    )(spot, own, other)


def dot_e(left, right, dims):
    return dot3(halves(left), halves(right), dims)


def solve_kernel(spot_ref, *refs, block, last, panel):
    refs = list(refs)
    y, core = spot_ref[3], spot_ref[4]
    take = lambda: refs.pop(0)
    grads_ref = take()
    known = []
    if block == 0:
        x = take()[...]
        solved = dot_e(x, grads_ref[0:panel, :], NN)
        v = dot_e(x, solved, TN)
    else:
        shares = [take()[...] for _ in range(4)]
        inverse_ref = take()
        lead = 2 * (block % 2)
        near = y == lead
        twin = y == lead + 1
        far = y == (lead ^ 2)
        upper = jnp.where(near, shares[0], jnp.where(twin, shares[1], jnp.where(far, shares[2], shares[3])))
        lower = jnp.where(twin, shares[0], jnp.where(near, shares[1], jnp.where(far, shares[3], shares[2])))
        right = jnp.concatenate([upper, lower], axis=0)
        solved = dot_e(inverse_ref[0], right, NN)
        if last:
            refs[0][...] = solved
            return
        square_ref, panel_ref, v_ref = take(), take(), take()
        known = [take()[...] for _ in range(block - 1)] + [solved]
        v = v_ref[...] - dot_e(square_ref[...], dot_e(panel_ref[...], solved, NN), NN)
    own_ref, other_ref = take(), take()
    solved_ref, v_out, share_ref = refs
    tile = panel // 2
    part = tile // 2
    slot = (block + 1) // 2
    rest = []
    for ref in (own_ref, other_ref):
        total = dot_e(ref[:, :panel], v, NN)
        for j, value in enumerate(known):
            total = total + dot_e(ref[:, (j + 1) * panel : (j + 2) * panel], value, NN)
        rest.append(total)
    start = (slot * 4 + y) * tile
    for value, side in ((rest[0], core), (rest[1], 1 - core)):
        at = pl.multiple_of(side * part, part)
        row = pl.multiple_of(start + at, part)
        share_ref[pl.ds(at, part), :] = grads_ref[pl.ds(row, part), :] - value
    solved_ref[...] = solved
    v_out[...] = v


def forward_solve(spot, x, square, grads, inverses, panels, own, other):
    panel = x.shape[0]
    count = grads.shape[1]
    blocks = grads.shape[0] // panel
    solved, v, share = [], None, None
    for block in range(blocks):
        last = block == blocks - 1
        operands, specs = [spot, grads], [SMEM, VMEM]
        if block == 0:
            operands += [x]
            specs += [VMEM]
        else:
            got = [share] + [swap(share, dy=m, only=on_line) for m in (1, 2, 3)]
            operands += [*got, inverses]
            specs += [VMEM] * 4
            specs += [pl.BlockSpec((1, panel, panel), lambda i, b=block: (b - 1, 0, 0))]
            if not last:
                operands += [square, panels, v, *solved[1:]]
                specs += [VMEM, pl.BlockSpec((panel, panel), lambda i, b=block: (0, b))]
                specs += [VMEM] * block
        if not last:
            slot = (block + 1) // 2
            operands += [own[slot], other[slot]]
            specs += [VMEM, VMEM]
        outs = [shape(panel, count)]
        if not last:
            outs += [shape(panel, count), shape(panel // 2, count)]
        run = pl.pallas_call(
            functools.partial(solve_kernel, block=block, last=last, panel=panel),
            out_shape=outs,
            grid=(1,),
            in_specs=specs,
            out_specs=[VMEM] * len(outs),
            interpret=INTERPRET,
            name="solve",
        )
        result = run(*operands)
        solved.append(result[0])
        if not last:
            v, share = result[1], result[2]
    return solved


def spread_solution(spot, solved, z, x, y, core):
    whole = jnp.concatenate(solved, axis=0)
    rows = whole.shape[0]
    own = lax.dynamic_slice_in_dim(whole, (y * 2 + core) * (rows // 8), rows // 8, 0)
    got = [swap(own, dx=d, only=on_line) for d in (1, 2, 3)]
    own = jnp.where(x == 2, own, got[0] + got[1] + got[2])
    source = lambda zz, xx, yy, cc: zz == 0
    got = [swap(own, dz=d, only=source) for d in (1, 2, 3)]
    own = jnp.where(z == 0, own, got[0] + got[1] + got[2])
    lines = jnp.stack([own] + [swap(own, dy=d) for d in (1, 2, 3)])
    other = swap(lines, dcore=1)
    return pl.pallas_call(
        place_rows_kernel,
        out_shape=shape(*whole.shape),
        in_specs=[SMEM, VMEM, VMEM],
        out_specs=VMEM,
        interpret=INTERPRET,
        name="place_rows",
    )(spot, lines, other)


def place_rows_kernel(spot_ref, own_ref, other_ref, out_ref):
    rows = own_ref.shape[1]
    y, core = spot_ref[3], spot_ref[4]
    for ref, side in ((own_ref, core), (other_ref, 1 - core)):
        for m in range(4):
            at = ((y ^ m) * 2 + side) * rows
            out_ref[pl.ds(pl.multiple_of(at, rows), rows), :] = ref[m]


def program(factor, damping, gradients, inverses):
    part, order = factor.shape
    panel_width = inverses.shape[1]
    z, xh, xl = lax.axis_index("z"), lax.axis_index("xh"), lax.axis_index("xl")
    y, core = lax.axis_index("y"), lax.axis_index("core")
    x = xh * 2 + xl
    spot = jnp.stack([z, xh, xl, y, core]).astype(jnp.int32)
    device = device_of(z, xh, xl, y, core)
    panel = factor[:, :panel_width]
    row = lax.broadcasted_iota(jnp.int32, panel.shape, 0) + device * part
    col = lax.broadcasted_iota(jnp.int32, panel.shape, 1)
    panel = panel + jnp.where(row == col, damping[:, None], 0.0)

    from_first = lambda zz, xx, yy, cc: zz == 0 and xx == 0
    from_second = lambda zz, xx, yy, cc: zz == 0 and xx == 1
    lead = [swap(panel, dx=2, only=from_first), swap(panel, dx=3, only=from_second), panel]
    got = corner_lines(panel)
    rows_share = share_rows(panel)
    cols_share = share_cols(panel)
    corner_own = corner_both(panel, got, y)
    corner_other = swap(corner_own, dcore=1, only=from_first)
    ends = jnp.where(y < 2, lead[2], lead[0])
    ends = jnp.concatenate([lead[1], ends], axis=0)
    lines = jnp.stack([ends] + [swap(ends, dy=m, only=on_line) for m in (1, 2, 3)])
    lines_other = swap(lines, dcore=1, only=on_line)
    pieces = spread_corner(corner_own, corner_other, z, x)
    rows_in = lax.all_gather(rows_share, ("xl", "y", "core"), tiled=True)
    cols_in = lax.all_gather(cols_share, ("z", "xh"), tiled=True)
    second = swap(factor[:, panel_width : 3 * panel_width], dx=3, only=from_second)
    lower = [
        lead[0],
        jnp.concatenate([lead[1], second], axis=1),
        factor[:, : 5 * panel_width],
    ]
    lower_other = [swap(value, dcore=1, only=on_line) for value in lower]

    stages = [send_chunk(spot, factor, damping[None, :], chunk, ()) for chunk in range(CHUNKS)]

    x_inverse, inverse = inverse_factor(spot, pieces)
    panels = place_panels(spot, lines, lines_other)
    row_factor, col_factor, tiles = panel_solve(spot, x_inverse, rows_in, cols_in)

    solved = forward_solve(spot, x_inverse, inverse, gradients, inverses, panels, lower, lower_other)
    solution_rows = spread_solution(spot, solved, z, x, y, core)

    out = None
    for chunk in range(CHUNKS):
        out = update(spot, stages[chunk], row_factor, col_factor, out, chunk)
    tile = order // 64
    updated = out.reshape(8, 1, tile, 4, 1, tile)
    panel_tiles = tiles.reshape(8, 1, part // 8, panel_width)
    return (updated, panel_tiles, solution_rows)


def solution(mesh):
    split = Mesh(mesh.devices.reshape(4, 2, 2, 4, 2), ALL)
    row, col = ("z", "xh"), ("xl", "y", "core")
    return jax.shard_map(
        program,
        mesh=split,
        in_specs=(P(row + col, None), P(row + col), P(), P()),
        out_specs=(P(None, row, None, None, col, None), P(None, row, col, None), P()),
        check_vma=False,
    )
```

```python
import functools

import jax
import jax.numpy as jnp
from jax import lax
from jax.experimental import pallas as pl
from jax.experimental.pallas import tpu as pltpu
from jax.sharding import Mesh
from jax.sharding import PartitionSpec as P


INTERPRET = False
ALL = ("z", "xh", "xl", "y", "core")
VMEM = pl.BlockSpec(memory_space=pltpu.VMEM)
SMEM = pl.BlockSpec(memory_space=pltpu.SMEM)
ANY = pl.BlockSpec(memory_space=pl.ANY)
F32 = jnp.float32


def shape(*dims):
    return jax.ShapeDtypeStruct(dims, F32)


def dot(left, right, dims):
    return lax.dot_general(
        left, right, (dims, ((), ())), precision=lax.Precision.HIGHEST, preferred_element_type=F32
    )


def halves(value):
    high = value.astype(jnp.bfloat16)
    return high, (value - high.astype(F32)).astype(jnp.bfloat16)


def dot3(left, right, dims):
    one = lambda a, b: lax.dot_general(a, b, (dims, ((), ())), preferred_element_type=F32)
    return one(left[0], right[0]) + (one(left[0], right[1]) + one(left[1], right[0]))


NN = ((1,), (0,))
NT = ((1,), (1,))
TN = ((0,), (0,))


def device_of(z, xh, xl, y, core):
    return (((z * 2 + xh) * 2 + xl) * 4 + y) * 2 + core


def every():
    return [
        (z, xh, xl, y, core)
        for z in range(4)
        for xh in range(2)
        for xl in range(2)
        for y in range(4)
        for core in range(2)
    ]


def swap(value, dz=0, dx=0, dy=0, dcore=0, only=None):
    pairs = []
    for z, xh, xl, y, core in every():
        if only is None or only(z, xh * 2 + xl, y, core):
            to = (z ^ dz, xh ^ (dx >> 1), xl ^ (dx & 1), y ^ dy, core ^ dcore)
            pairs.append((device_of(z, xh, xl, y, core), device_of(*to)))
    return lax.ppermute(value, ALL, pairs)


def factor_block(block):
    size = block.shape[0]
    lane = lax.broadcasted_iota(jnp.int32, (8, size), 1)
    sub = lax.broadcasted_iota(jnp.int32, (8, size), 0)
    left = [block[8 * i : 8 * i + 8, :] for i in range(size // 8)]
    right = [jnp.where(lane == sub + 8 * i, 1.0, 0.0).astype(F32) for i in range(size // 8)]
    for k in range(size - 1):
        b, s = divmod(k, 8)
        inverse = 1.0 / left[b][s : s + 1, k : k + 1]
        left_row = jnp.broadcast_to(left[b][s : s + 1, :] * inverse, (8, size))
        right_row = jnp.broadcast_to(right[b][s : s + 1, :] * inverse, (8, size))
        for i in range(b if s < 7 else b + 1, size // 8):
            col = jnp.broadcast_to(left[i][:, k : k + 1], (8, size))
            if i == b:
                col = jnp.where(sub > s, col, 0.0)
            left[i] = left[i] - col * left_row
            right[i] = right[i] - col * right_row
    rows = []
    for i in range(size // 8):
        pivot = jnp.sum(jnp.where(lane == sub + 8 * i, left[i], 0.0), axis=1, keepdims=True)
        rows.append(right[i] * (1.0 / jnp.sqrt(pivot)))
    return jnp.concatenate(rows, axis=0)


def corner_kernel(spot_ref, *refs):
    pieces = refs[:4]
    x_ref, square_ref, w_ref = refs[-3:]
    n = x_ref.shape[0]
    nb = n // 4
    part = pieces[0].shape[1]
    z = spot_ref[0]
    core = spot_ref[4]
    for q in range(4):
        for i in range(4):
            side = core if i < 2 else 1 - core
            row = pl.multiple_of((i % 2) * (n // 2) + side * (n // 4) + (z ^ q) * part, part)
            w_ref[pl.ds(row, part), :] = pieces[q][i]
    ri = lax.broadcasted_iota(jnp.int32, (n, n), 0)
    ci = lax.broadcasted_iota(jnp.int32, (n, n), 1)
    x_ref[...] = jnp.where(ri == ci, 1.0, 0.0).astype(F32)

    def step(j, carry):
        at = pl.multiple_of(j * nb, nb)
        xj = factor_block(w_ref[pl.ds(at, nb), pl.ds(at, nb)])
        low = dot(w_ref[:, pl.ds(at, nb)], xj, NT)
        rows = lax.broadcasted_iota(jnp.int32, (n, nb), 0)
        low = jnp.where(rows >= at + nb, low, 0.0)
        w_ref[...] = w_ref[...] - dot(low, low, NT)
        xr = dot(xj, x_ref[pl.ds(at, nb), :], NN)
        x_ref[pl.ds(at, nb), :] = xr
        x_ref[...] = x_ref[...] - dot(low, xr, NN)
        return carry

    lax.fori_loop(0, 4, step, 0)
    x = x_ref[...]
    square_ref[...] = dot(x, x, TN)


def inverse_factor(spot, pieces):
    n = pieces[0].shape[2]
    return pl.pallas_call(
        corner_kernel,
        out_shape=[shape(n, n), shape(n, n)],
        in_specs=[SMEM] + [VMEM] * 4,
        out_specs=[VMEM, VMEM],
        scratch_shapes=[pltpu.VMEM((n, n), F32)],
        interpret=INTERPRET,
        name="inverse_factor",
    )(spot, *pieces)


def corner_lines(panel):
    source = lambda zz, xx, yy, cc: zz == 0 and xx == 0 and yy < 2
    return [swap(panel, dy=d, only=source) for d in (1, 2, 3)]


def corner_both(panel, got, y):
    upper = jnp.where(y == 0, panel, jnp.where(y == 1, got[0], jnp.where(y == 2, got[1], got[2])))
    lower = jnp.where(y == 1, panel, jnp.where(y == 0, got[0], jnp.where(y == 3, got[1], got[2])))
    return jnp.stack([upper, lower])


def spread_corner(own, other, z, x):
    whole = jnp.concatenate([own, other], axis=0)
    part = whole.shape[1] // 4
    pieces = [whole[:, d * part : (d + 1) * part] for d in range(4)]
    first = lambda zz, xx, yy, cc: zz == 0 and xx == 0
    got = [swap(pieces[d], dz=d, only=first) for d in (1, 2, 3)]
    value = jnp.where(z == 0, pieces[0], got[0] + got[1] + got[2])
    second = lambda zz, xx, yy, cc: xx == 0
    got = [swap(value, dx=d, only=second) for d in (1, 2, 3)]
    value = jnp.where(x == 0, value, got[0] + got[1] + got[2])
    return [value] + [swap(value, dz=d) for d in (1, 2, 3)]


def pack_kernel(spot_ref, factor_ref, damping_ref, out_ref, hold):
    rows = hold.shape[0]
    part = damping_ref.shape[1]
    count, _, cols = out_ref.shape
    width = cols // 4
    z, xh, xl, y, core = (spot_ref[i] for i in range(5))
    hold[...] = factor_ref[...]
    device = (((z * 2 + xh) * 2 + xl) * 4 + y) * 2 + core
    at = pl.multiple_of(device * part, part)
    lane = lax.broadcasted_iota(jnp.int32, (rows, part), 1)
    sub = lax.broadcasted_iota(jnp.int32, (rows, part), 0)
    damping = jnp.broadcast_to(damping_ref[...], (rows, part))
    add = jnp.where(lane == sub + pl.program_id(0) * rows, damping, 0.0)
    hold[:, pl.ds(at, part)] = hold[:, pl.ds(at, part)] + add
    for m in range(count):
        for b in range(4):
            col = b * count + m
            out_ref[m, :, b * width : (b + 1) * width] = hold[:, col * width : (col + 1) * width]


def send_tiles(spot, factor, damping):
    part, order = factor.shape
    rows = part // 4
    cols = order // 16
    packed = pl.pallas_call(
        pack_kernel,
        out_shape=shape(16, part, cols),
        grid=(4,),
        in_specs=[SMEM, pl.BlockSpec((rows, order), lambda i: (i, 0)), VMEM],
        out_specs=pl.BlockSpec((16, rows, cols), lambda i: (0, i, 0)),
        scratch_shapes=[pltpu.VMEM((rows, order), F32)],
        interpret=INTERPRET,
        name="pack_tiles",
    )(spot, factor, damping)
    packed = lax.all_to_all(packed, ("xl", "y", "core"), 0, 0, tiled=True)
    return lax.all_to_all(packed.reshape(8, 2 * part, cols), ("z", "xh"), 0, 0, tiled=True)


def panel_kernel(spot_ref, x_ref, rows_ref, cols_ref, row_ref, col_ref, tile_ref):
    part = rows_ref.shape[0] // 16
    xl, y, core = spot_ref[2], spot_ref[3], spot_ref[4]
    x = halves(x_ref[...])
    row_ref[...] = dot3(halves(rows_ref[...]), x, NT)
    col_ref[...] = dot3(halves(cols_ref[...]), x, NT)
    share = part // 8
    column = (xl * 4 + y) * 2 + core
    for a in range(8):
        at = pl.multiple_of(a * 2 * part + column * share, share)
        tile_ref[a * share : (a + 1) * share, :] = row_ref[pl.ds(at, share), :]


def panel_solve(spot, x, rows_in, cols_in):
    width = x.shape[0]
    return pl.pallas_call(
        panel_kernel,
        out_shape=[shape(*rows_in.shape), shape(*cols_in.shape), shape(rows_in.shape[0] // 16, width)],
        in_specs=[SMEM, VMEM, VMEM, VMEM],
        out_specs=[VMEM] * 3,
        interpret=INTERPRET,
        name="panel_solve",
    )(spot, x, rows_in, cols_in)


def share_rows(panel):
    pairs = []
    for z, xh, xl, y, core in every():
        to = (xl * 2 + (y >> 1), y & 1, z >> 1, (z & 1) * 2 + xh, core)
        pairs.append((device_of(z, xh, xl, y, core), device_of(*to)))
    return lax.ppermute(panel, ALL, pairs)


def share_cols(panel):
    pairs = []
    for z, xh, xl, y, core in every():
        to = (z, core, xh, xl * 2 + (y >> 1), y & 1)
        pairs.append((device_of(z, xh, xl, y, core), device_of(*to)))
    return lax.ppermute(panel, ALL, pairs)


def update_kernel(block_ref, row_ref, col_ref, out_ref, high_ref, low_ref, hold):
    @pl.when(pl.program_id(0) == 0)
    def _():
        high_ref[...], low_ref[...] = halves(col_ref[...])

    left = halves(row_ref[...])
    hold[...] = block_ref[0] - dot3(left, (high_ref[...], low_ref[...]), NT)
    rows, cols = hold.shape
    lanes = out_ref.shape[1]
    groups = cols // lanes
    for g in range(groups):
        out_ref[pl.ds(g, rows, stride=groups), :] = hold[:, g * lanes : (g + 1) * lanes]


def update(blocks, row_factor, col_factor):
    count, rows, cols = blocks.shape
    width = row_factor.shape[1]
    lanes = cols // 8
    return pl.pallas_call(
        update_kernel,
        out_shape=shape(count * rows * 8, lanes),
        grid=(count,),
        in_specs=[
            pl.BlockSpec((1, rows, cols), lambda i: (i, 0, 0)),
            pl.BlockSpec((rows, width), lambda i: (i, 0)),
            pl.BlockSpec(col_factor.shape, lambda i: (0, 0)),
        ],
        out_specs=pl.BlockSpec((rows * 8, lanes), lambda i: (i, 0)),
        scratch_shapes=[
            pltpu.VMEM(col_factor.shape, jnp.bfloat16),
            pltpu.VMEM(col_factor.shape, jnp.bfloat16),
            pltpu.VMEM((rows, cols), F32),
        ],
        interpret=INTERPRET,
        name="update",
    )(blocks, row_factor, col_factor)


def on_line(z, x, y, core):
    return z == 0 and x == 2


def place_panels_kernel(spot_ref, own_ref, other_ref, out_ref):
    part = own_ref.shape[1] // 2
    y, core = spot_ref[3], spot_ref[4]
    for ref, side in ((own_ref, core), (other_ref, 1 - core)):
        for m in range(4):
            line = y ^ m
            for slot, tile in ((0, 4 + line), (1, line + 8 * (1 - line // 2))):
                at = (tile * 2 + side) * part
                out_ref[:, pl.ds(pl.multiple_of(at, part), part)] = ref[
                    m, slot * part : (slot + 1) * part, :
                ].T


def place_panels(spot, own, other):
    _, rows, width = own.shape
    return pl.pallas_call(
        place_panels_kernel,
        out_shape=shape(width, 12 * rows),
        in_specs=[SMEM, VMEM, VMEM],
        out_specs=VMEM,
        interpret=INTERPRET,
        name="place_panels",
    )(spot, own, other)


def dot_e(left, right, dims):
    return dot3(halves(left), halves(right), dims)


def solve_kernel(spot_ref, *refs, block, last, panel):
    refs = list(refs)
    y, core = spot_ref[3], spot_ref[4]
    take = lambda: refs.pop(0)
    grads_ref = take()
    known = []
    if block == 0:
        x = take()[...]
        solved = dot_e(x, grads_ref[0:panel, :], NN)
        v = dot_e(x, solved, TN)
    else:
        shares = [take()[...] for _ in range(4)]
        inverse_ref = take()
        lead = 2 * (block % 2)
        near = y == lead
        twin = y == lead + 1
        far = y == (lead ^ 2)
        upper = jnp.where(near, shares[0], jnp.where(twin, shares[1], jnp.where(far, shares[2], shares[3])))
        lower = jnp.where(twin, shares[0], jnp.where(near, shares[1], jnp.where(far, shares[3], shares[2])))
        right = jnp.concatenate([upper, lower], axis=0)
        solved = dot_e(inverse_ref[0], right, NN)
        if last:
            refs[0][...] = solved
            return
        square_ref, panel_ref, v_ref = take(), take(), take()
        known = [take()[...] for _ in range(block - 1)] + [solved]
        v = v_ref[...] - dot_e(square_ref[...], dot_e(panel_ref[...], solved, NN), NN)
    own_ref, other_ref = take(), take()
    solved_ref, v_out, share_ref = refs
    tile = panel // 2
    part = tile // 2
    slot = (block + 1) // 2
    rest = []
    for ref in (own_ref, other_ref):
        total = dot_e(ref[:, :panel], v, NN)
        for j, value in enumerate(known):
            total = total + dot_e(ref[:, (j + 1) * panel : (j + 2) * panel], value, NN)
        rest.append(total)
    start = (slot * 4 + y) * tile
    for value, side in ((rest[0], core), (rest[1], 1 - core)):
        at = pl.multiple_of(side * part, part)
        row = pl.multiple_of(start + at, part)
        share_ref[pl.ds(at, part), :] = grads_ref[pl.ds(row, part), :] - value
    solved_ref[...] = solved
    v_out[...] = v


def forward_solve(spot, x, square, grads, inverses, panels, own, other):
    panel = x.shape[0]
    count = grads.shape[1]
    blocks = grads.shape[0] // panel
    solved, v, share = [], None, None
    for block in range(blocks):
        last = block == blocks - 1
        operands, specs = [spot, grads], [SMEM, VMEM]
        if block == 0:
            operands += [x]
            specs += [VMEM]
        else:
            got = [share] + [swap(share, dy=m, only=on_line) for m in (1, 2, 3)]
            operands += [*got, inverses]
            specs += [VMEM] * 4
            specs += [pl.BlockSpec((1, panel, panel), lambda i, b=block: (b - 1, 0, 0))]
            if not last:
                operands += [square, panels, v, *solved[1:]]
                specs += [VMEM, pl.BlockSpec((panel, panel), lambda i, b=block: (0, b))]
                specs += [VMEM] * block
        if not last:
            slot = (block + 1) // 2
            operands += [own[slot], other[slot]]
            specs += [VMEM, VMEM]
        outs = [shape(panel, count)]
        if not last:
            outs += [shape(panel, count), shape(panel // 2, count)]
        run = pl.pallas_call(
            functools.partial(solve_kernel, block=block, last=last, panel=panel),
            out_shape=outs,
            grid=(1,),
            in_specs=specs,
            out_specs=[VMEM] * len(outs),
            interpret=INTERPRET,
            name="solve",
        )
        result = run(*operands)
        solved.append(result[0])
        if not last:
            v, share = result[1], result[2]
    return solved


def spread_solution(spot, solved, z, x, y, core):
    whole = jnp.concatenate(solved, axis=0)
    rows = whole.shape[0]
    own = lax.dynamic_slice_in_dim(whole, (y * 2 + core) * (rows // 8), rows // 8, 0)
    got = [swap(own, dx=d, only=on_line) for d in (1, 2, 3)]
    own = jnp.where(x == 2, own, got[0] + got[1] + got[2])
    source = lambda zz, xx, yy, cc: zz == 0
    got = [swap(own, dz=d, only=source) for d in (1, 2, 3)]
    own = jnp.where(z == 0, own, got[0] + got[1] + got[2])
    lines = jnp.stack([own] + [swap(own, dy=d) for d in (1, 2, 3)])
    other = swap(lines, dcore=1)
    return pl.pallas_call(
        place_rows_kernel,
        out_shape=shape(*whole.shape),
        in_specs=[SMEM, VMEM, VMEM],
        out_specs=VMEM,
        interpret=INTERPRET,
        name="place_rows",
    )(spot, lines, other)


def place_rows_kernel(spot_ref, own_ref, other_ref, out_ref):
    rows = own_ref.shape[1]
    y, core = spot_ref[3], spot_ref[4]
    for ref, side in ((own_ref, core), (other_ref, 1 - core)):
        for m in range(4):
            at = ((y ^ m) * 2 + side) * rows
            out_ref[pl.ds(pl.multiple_of(at, rows), rows), :] = ref[m]


def program(factor, damping, gradients, inverses):
    part, order = factor.shape
    panel_width = inverses.shape[1]
    z, xh, xl = lax.axis_index("z"), lax.axis_index("xh"), lax.axis_index("xl")
    y, core = lax.axis_index("y"), lax.axis_index("core")
    x = xh * 2 + xl
    spot = jnp.stack([z, xh, xl, y, core]).astype(jnp.int32)
    device = device_of(z, xh, xl, y, core)
    panel = factor[:, :panel_width]
    row = lax.broadcasted_iota(jnp.int32, panel.shape, 0) + device * part
    col = lax.broadcasted_iota(jnp.int32, panel.shape, 1)
    panel = panel + jnp.where(row == col, damping[:, None], 0.0)

    from_first = lambda zz, xx, yy, cc: zz == 0 and xx == 0
    from_second = lambda zz, xx, yy, cc: zz == 0 and xx == 1
    got = corner_lines(panel)
    lead = [swap(panel, dx=2, only=from_first), swap(panel, dx=3, only=from_second), panel]
    second = swap(factor[:, panel_width : 3 * panel_width], dx=3, only=from_second)
    corner_own = corner_both(panel, got, y)
    corner_other = swap(corner_own, dcore=1, only=from_first)
    rows_share = share_rows(panel)
    cols_share = share_cols(panel)
    pieces = spread_corner(corner_own, corner_other, z, x)
    rows_in = lax.all_gather(rows_share, ("xl", "y", "core"), tiled=True)
    cols_in = lax.all_gather(cols_share, ("z", "xh"), tiled=True)
    blocks = send_tiles(spot, factor, damping[None, :])

    ends = jnp.where(y < 2, lead[2], lead[0])
    ends = jnp.concatenate([lead[1], ends], axis=0)
    lines = jnp.stack([ends] + [swap(ends, dy=m, only=on_line) for m in (1, 2, 3)])
    lower = [
        lead[0],
        jnp.concatenate([lead[1], second], axis=1),
        factor[:, : 5 * panel_width],
    ]
    lower_other = [swap(value, dcore=1, only=on_line) for value in lower]
    lines_other = swap(lines, dcore=1, only=on_line)

    x_inverse, inverse = inverse_factor(spot, pieces)
    panels = place_panels(spot, lines, lines_other)
    row_factor, col_factor, tiles = panel_solve(spot, x_inverse, rows_in, cols_in)

    solved = forward_solve(spot, x_inverse, inverse, gradients, inverses, panels, lower, lower_other)
    solution_rows = spread_solution(spot, solved, z, x, y, core)

    out = update(blocks, row_factor, col_factor)
    tile = order // 64
    updated = out.reshape(8, 1, tile, 4, 1, tile)
    panel_tiles = tiles.reshape(8, 1, part // 8, panel_width)
    return (updated, panel_tiles, solution_rows)


def solution(mesh):
    split = Mesh(mesh.devices.reshape(4, 2, 2, 4, 2), ALL)
    row, col = ("z", "xh"), ("xl", "y", "core")
    return jax.shard_map(
        program,
        mesh=split,
        in_specs=(P(row + col, None), P(row + col), P(), P()),
        out_specs=(P(None, row, None, None, col, None), P(None, row, col, None), P()),
        check_vma=False,
    )
```

```python
import functools

import jax
import jax.numpy as jnp
from jax import lax
from jax.experimental import pallas as pl
from jax.experimental.pallas import tpu as pltpu
from jax.sharding import Mesh
from jax.sharding import PartitionSpec as P


INTERPRET = False
ALL = ("z", "xh", "xl", "y", "core")
VMEM = pl.BlockSpec(memory_space=pltpu.VMEM)
SMEM = pl.BlockSpec(memory_space=pltpu.SMEM)
ANY = pl.BlockSpec(memory_space=pl.ANY)
F32 = jnp.float32


def shape(*dims):
    return jax.ShapeDtypeStruct(dims, F32)


def dot(left, right, dims):
    return lax.dot_general(
        left, right, (dims, ((), ())), precision=lax.Precision.HIGHEST, preferred_element_type=F32
    )


def halves(value):
    high = value.astype(jnp.bfloat16)
    return high, (value - high.astype(F32)).astype(jnp.bfloat16)


def dot3(left, right, dims):
    one = lambda a, b: lax.dot_general(a, b, (dims, ((), ())), preferred_element_type=F32)
    return one(left[0], right[0]) + (one(left[0], right[1]) + one(left[1], right[0]))


NN = ((1,), (0,))
NT = ((1,), (1,))
TN = ((0,), (0,))


def device_of(z, xh, xl, y, core):
    return (((z * 2 + xh) * 2 + xl) * 4 + y) * 2 + core


def every():
    return [
        (z, xh, xl, y, core)
        for z in range(4)
        for xh in range(2)
        for xl in range(2)
        for y in range(4)
        for core in range(2)
    ]


def swap(value, dz=0, dx=0, dy=0, dcore=0, only=None):
    pairs = []
    for z, xh, xl, y, core in every():
        if only is None or only(z, xh * 2 + xl, y, core):
            to = (z ^ dz, xh ^ (dx >> 1), xl ^ (dx & 1), y ^ dy, core ^ dcore)
            pairs.append((device_of(z, xh, xl, y, core), device_of(*to)))
    return lax.ppermute(value, ALL, pairs)


def factor_block(block):
    size = block.shape[0]
    lane = lax.broadcasted_iota(jnp.int32, (8, size), 1)
    sub = lax.broadcasted_iota(jnp.int32, (8, size), 0)
    left = [block[8 * i : 8 * i + 8, :] for i in range(size // 8)]
    right = [jnp.where(lane == sub + 8 * i, 1.0, 0.0).astype(F32) for i in range(size // 8)]
    for k in range(size - 1):
        b, s = divmod(k, 8)
        inverse = 1.0 / left[b][s : s + 1, k : k + 1]
        left_row = jnp.broadcast_to(left[b][s : s + 1, :] * inverse, (8, size))
        right_row = jnp.broadcast_to(right[b][s : s + 1, :] * inverse, (8, size))
        for i in range(b if s < 7 else b + 1, size // 8):
            col = jnp.broadcast_to(left[i][:, k : k + 1], (8, size))
            if i == b:
                col = jnp.where(sub > s, col, 0.0)
            left[i] = left[i] - col * left_row
            right[i] = right[i] - col * right_row
    rows = []
    for i in range(size // 8):
        pivot = jnp.sum(jnp.where(lane == sub + 8 * i, left[i], 0.0), axis=1, keepdims=True)
        rows.append(right[i] * (1.0 / jnp.sqrt(pivot)))
    return jnp.concatenate(rows, axis=0)


def corner_kernel(spot_ref, *refs):
    pieces = refs[:4]
    x_ref, square_ref, w_ref = refs[-3:]
    n = x_ref.shape[0]
    nb = n // 4
    part = pieces[0].shape[1]
    z = spot_ref[0]
    core = spot_ref[4]
    for q in range(4):
        for i in range(4):
            side = core if i < 2 else 1 - core
            row = pl.multiple_of((i % 2) * (n // 2) + side * (n // 4) + (z ^ q) * part, part)
            w_ref[pl.ds(row, part), :] = pieces[q][i]
    ri = lax.broadcasted_iota(jnp.int32, (n, n), 0)
    ci = lax.broadcasted_iota(jnp.int32, (n, n), 1)
    x_ref[...] = jnp.where(ri == ci, 1.0, 0.0).astype(F32)

    def step(j, carry):
        at = pl.multiple_of(j * nb, nb)
        xj = factor_block(w_ref[pl.ds(at, nb), pl.ds(at, nb)])
        low = dot(w_ref[:, pl.ds(at, nb)], xj, NT)
        rows = lax.broadcasted_iota(jnp.int32, (n, nb), 0)
        low = jnp.where(rows >= at + nb, low, 0.0)
        w_ref[...] = w_ref[...] - dot(low, low, NT)
        xr = dot(xj, x_ref[pl.ds(at, nb), :], NN)
        x_ref[pl.ds(at, nb), :] = xr
        x_ref[...] = x_ref[...] - dot(low, xr, NN)
        return carry

    lax.fori_loop(0, 4, step, 0)
    x = x_ref[...]
    square_ref[...] = dot(x, x, TN)


def inverse_factor(spot, pieces):
    n = pieces[0].shape[2]
    return pl.pallas_call(
        corner_kernel,
        out_shape=[shape(n, n), shape(n, n)],
        in_specs=[SMEM] + [VMEM] * 4,
        out_specs=[VMEM, VMEM],
        scratch_shapes=[pltpu.VMEM((n, n), F32)],
        interpret=INTERPRET,
        name="inverse_factor",
    )(spot, *pieces)


def spread_corner(panel, z, x, y):
    part = panel.shape[0] // 4
    pieces = [panel[d * part : (d + 1) * part] for d in range(4)]
    source = lambda zz, xx, yy, cc: zz == 0 and xx == 0 and yy < 2
    got = [swap(pieces[d], dz=d, only=source) for d in (1, 2, 3)]
    value = jnp.where(z == 0, pieces[0], got[0] + got[1] + got[2])
    source = lambda zz, xx, yy, cc: xx == 0 and yy < 2
    got = [swap(value, dx=d, only=source) for d in (1, 2, 3)]
    value = jnp.where(x == 0, value, got[0] + got[1] + got[2])
    source = lambda zz, xx, yy, cc: yy < 2
    got = [swap(value, dy=d, only=source) for d in (1, 2, 3)]
    upper = jnp.where(y == 0, value, jnp.where(y == 1, got[0], jnp.where(y == 2, got[1], got[2])))
    lower = jnp.where(y == 1, value, jnp.where(y == 0, got[0], jnp.where(y == 3, got[1], got[2])))
    both = jnp.stack([upper, lower])
    value = jnp.concatenate([both, swap(both, dcore=1)], axis=0)
    return [value] + [swap(value, dz=d) for d in (1, 2, 3)]


def pack_kernel(spot_ref, factor_ref, damping_ref, out_ref, hold):
    rows = hold.shape[0]
    part = damping_ref.shape[1]
    count, _, cols = out_ref.shape
    width = cols // 4
    z, xh, xl, y, core = (spot_ref[i] for i in range(5))
    hold[...] = factor_ref[...]
    device = (((z * 2 + xh) * 2 + xl) * 4 + y) * 2 + core
    at = pl.multiple_of(device * part, part)
    lane = lax.broadcasted_iota(jnp.int32, (rows, part), 1)
    sub = lax.broadcasted_iota(jnp.int32, (rows, part), 0)
    damping = jnp.broadcast_to(damping_ref[...], (rows, part))
    add = jnp.where(lane == sub + pl.program_id(0) * rows, damping, 0.0)
    hold[:, pl.ds(at, part)] = hold[:, pl.ds(at, part)] + add
    for m in range(count):
        for b in range(4):
            col = b * count + m
            out_ref[m, :, b * width : (b + 1) * width] = hold[:, col * width : (col + 1) * width]


def send_tiles(spot, factor, damping):
    part, order = factor.shape
    rows = part // 4
    cols = order // 16
    packed = pl.pallas_call(
        pack_kernel,
        out_shape=shape(16, part, cols),
        grid=(4,),
        in_specs=[SMEM, pl.BlockSpec((rows, order), lambda i: (i, 0)), VMEM],
        out_specs=pl.BlockSpec((16, rows, cols), lambda i: (0, i, 0)),
        scratch_shapes=[pltpu.VMEM((rows, order), F32)],
        interpret=INTERPRET,
        name="pack_tiles",
    )(spot, factor, damping)
    packed = lax.all_to_all(packed, ("xl", "y", "core"), 0, 0, tiled=True)
    return lax.all_to_all(packed.reshape(8, 2 * part, cols), ("z", "xh"), 0, 0, tiled=True)


def panel_kernel(spot_ref, x_ref, rows_ref, cols_ref, row_ref, col_ref, tile_ref):
    part = rows_ref.shape[0] // 16
    xl, y, core = spot_ref[2], spot_ref[3], spot_ref[4]
    x = halves(x_ref[...])
    row_ref[...] = dot3(halves(rows_ref[...]), x, NT)
    col_ref[...] = dot3(halves(cols_ref[...]), x, NT)
    share = part // 8
    column = (xl * 4 + y) * 2 + core
    for a in range(8):
        at = pl.multiple_of(a * 2 * part + column * share, share)
        tile_ref[a * share : (a + 1) * share, :] = row_ref[pl.ds(at, share), :]


def panel_solve(spot, x, rows_in, cols_in):
    width = x.shape[0]
    return pl.pallas_call(
        panel_kernel,
        out_shape=[shape(*rows_in.shape), shape(*cols_in.shape), shape(rows_in.shape[0] // 16, width)],
        in_specs=[SMEM, VMEM, VMEM, VMEM],
        out_specs=[VMEM] * 3,
        interpret=INTERPRET,
        name="panel_solve",
    )(spot, x, rows_in, cols_in)


def share_rows(panel):
    pairs = []
    for z, xh, xl, y, core in every():
        to = (xl * 2 + (y >> 1), y & 1, z >> 1, (z & 1) * 2 + xh, core)
        pairs.append((device_of(z, xh, xl, y, core), device_of(*to)))
    return lax.ppermute(panel, ALL, pairs)


def share_cols(panel):
    pairs = []
    for z, xh, xl, y, core in every():
        to = (z, core, xh, xl * 2 + (y >> 1), y & 1)
        pairs.append((device_of(z, xh, xl, y, core), device_of(*to)))
    return lax.ppermute(panel, ALL, pairs)


def update_kernel(block_ref, row_ref, col_ref, *refs):
    out_ref, high_ref, low_ref, hold = refs[-4:]

    @pl.when(pl.program_id(0) == 0)
    def _():
        high_ref[...], low_ref[...] = halves(col_ref[...])

    left = halves(row_ref[...])
    hold[...] = block_ref[0] - dot3(left, (high_ref[...], low_ref[...]), NT)
    rows, cols = hold.shape
    lanes = out_ref.shape[1]
    groups = cols // lanes
    for g in range(groups):
        out_ref[pl.ds(g, rows, stride=groups), :] = hold[:, g * lanes : (g + 1) * lanes]


def update(blocks, row_factor, col_factor, out):
    count, rows, cols = blocks.shape
    half = count // 2
    first = 0 if out is None else half
    width = row_factor.shape[1]
    lanes = cols // 8
    return pl.pallas_call(
        update_kernel,
        out_shape=shape(count * rows * 8, lanes),
        grid=(half,),
        in_specs=[
            pl.BlockSpec((1, rows, cols), lambda i: (i + first, 0, 0)),
            pl.BlockSpec((rows, width), lambda i: (i + first, 0)),
            pl.BlockSpec(col_factor.shape, lambda i: (0, 0)),
        ]
        + ([] if out is None else [ANY]),
        out_specs=pl.BlockSpec((rows * 8, lanes), lambda i: (i + first, 0)),
        scratch_shapes=[
            pltpu.VMEM(col_factor.shape, jnp.bfloat16),
            pltpu.VMEM(col_factor.shape, jnp.bfloat16),
            pltpu.VMEM((rows, cols), F32),
        ],
        input_output_aliases={} if out is None else {3: 0},
        interpret=INTERPRET,
        name="update",
    )(blocks, row_factor, col_factor, *([] if out is None else [out]))


def on_line(z, x, y, core):
    return z == 0 and x == 2


def place_panels_kernel(spot_ref, own_ref, other_ref, out_ref):
    part = own_ref.shape[1] // 2
    y, core = spot_ref[3], spot_ref[4]
    for ref, side in ((own_ref, core), (other_ref, 1 - core)):
        for m in range(4):
            line = y ^ m
            for slot, tile in ((0, 4 + line), (1, line + 8 * (1 - line // 2))):
                at = (tile * 2 + side) * part
                out_ref[:, pl.ds(pl.multiple_of(at, part), part)] = ref[
                    m, slot * part : (slot + 1) * part, :
                ].T


def place_panels(spot, own, other):
    _, rows, width = own.shape
    return pl.pallas_call(
        place_panels_kernel,
        out_shape=shape(width, 12 * rows),
        in_specs=[SMEM, VMEM, VMEM],
        out_specs=VMEM,
        interpret=INTERPRET,
        name="place_panels",
    )(spot, own, other)


def dot_e(left, right, dims):
    return dot3(halves(left), halves(right), dims)


def solve_kernel(spot_ref, *refs, block, last, panel):
    refs = list(refs)
    y, core = spot_ref[3], spot_ref[4]
    take = lambda: refs.pop(0)
    grads_ref = take()
    known = []
    if block == 0:
        x = take()[...]
        solved = dot_e(x, grads_ref[0:panel, :], NN)
        v = dot_e(x, solved, TN)
    else:
        shares = [take()[...] for _ in range(4)]
        inverse_ref = take()
        lead = 2 * (block % 2)
        near = y == lead
        twin = y == lead + 1
        far = y == (lead ^ 2)
        upper = jnp.where(near, shares[0], jnp.where(twin, shares[1], jnp.where(far, shares[2], shares[3])))
        lower = jnp.where(twin, shares[0], jnp.where(near, shares[1], jnp.where(far, shares[3], shares[2])))
        right = jnp.concatenate([upper, lower], axis=0)
        solved = dot_e(inverse_ref[0], right, NN)
        if last:
            refs[0][...] = solved
            return
        square_ref, panel_ref, v_ref = take(), take(), take()
        known = [take()[...] for _ in range(block - 1)] + [solved]
        v = v_ref[...] - dot_e(square_ref[...], dot_e(panel_ref[...], solved, NN), NN)
    own_ref, other_ref = take(), take()
    solved_ref, v_out, share_ref = refs
    tile = panel // 2
    part = tile // 2
    slot = (block + 1) // 2
    rest = []
    for ref in (own_ref, other_ref):
        total = dot_e(ref[:, :panel], v, NN)
        for j, value in enumerate(known):
            total = total + dot_e(ref[:, (j + 1) * panel : (j + 2) * panel], value, NN)
        rest.append(total)
    start = (slot * 4 + y) * tile
    for value, side in ((rest[0], core), (rest[1], 1 - core)):
        at = pl.multiple_of(side * part, part)
        row = pl.multiple_of(start + at, part)
        share_ref[pl.ds(at, part), :] = grads_ref[pl.ds(row, part), :] - value
    solved_ref[...] = solved
    v_out[...] = v


def forward_solve(spot, x, square, grads, inverses, panels, own, other):
    panel = x.shape[0]
    count = grads.shape[1]
    blocks = grads.shape[0] // panel
    solved, v, share = [], None, None
    for block in range(blocks):
        last = block == blocks - 1
        operands, specs = [spot, grads], [SMEM, VMEM]
        if block == 0:
            operands += [x]
            specs += [VMEM]
        else:
            got = [share] + [swap(share, dy=m, only=on_line) for m in (1, 2, 3)]
            operands += [*got, inverses]
            specs += [VMEM] * 4
            specs += [pl.BlockSpec((1, panel, panel), lambda i, b=block: (b - 1, 0, 0))]
            if not last:
                operands += [square, panels, v, *solved[1:]]
                specs += [VMEM, pl.BlockSpec((panel, panel), lambda i, b=block: (0, b))]
                specs += [VMEM] * block
        if not last:
            slot = (block + 1) // 2
            operands += [own[slot], other[slot]]
            specs += [VMEM, VMEM]
        outs = [shape(panel, count)]
        if not last:
            outs += [shape(panel, count), shape(panel // 2, count)]
        run = pl.pallas_call(
            functools.partial(solve_kernel, block=block, last=last, panel=panel),
            out_shape=outs,
            grid=(1,),
            in_specs=specs,
            out_specs=[VMEM] * len(outs),
            interpret=INTERPRET,
            name="solve",
        )
        result = run(*operands)
        solved.append(result[0])
        if not last:
            v, share = result[1], result[2]
    return solved


def spread_solution(spot, solved, z, x, y, core):
    whole = jnp.concatenate(solved, axis=0)
    rows = whole.shape[0]
    own = lax.dynamic_slice_in_dim(whole, (y * 2 + core) * (rows // 8), rows // 8, 0)
    got = [swap(own, dx=d, only=on_line) for d in (1, 2, 3)]
    own = jnp.where(x == 2, own, got[0] + got[1] + got[2])
    source = lambda zz, xx, yy, cc: zz == 0
    got = [swap(own, dz=d, only=source) for d in (1, 2, 3)]
    own = jnp.where(z == 0, own, got[0] + got[1] + got[2])
    lines = jnp.stack([own] + [swap(own, dy=d) for d in (1, 2, 3)])
    other = swap(lines, dcore=1)
    return pl.pallas_call(
        place_rows_kernel,
        out_shape=shape(*whole.shape),
        in_specs=[SMEM, VMEM, VMEM],
        out_specs=VMEM,
        interpret=INTERPRET,
        name="place_rows",
    )(spot, lines, other)


def place_rows_kernel(spot_ref, own_ref, other_ref, out_ref):
    rows = own_ref.shape[1]
    y, core = spot_ref[3], spot_ref[4]
    for ref, side in ((own_ref, core), (other_ref, 1 - core)):
        for m in range(4):
            at = ((y ^ m) * 2 + side) * rows
            out_ref[pl.ds(pl.multiple_of(at, rows), rows), :] = ref[m]


def program(factor, damping, gradients, inverses):
    part, order = factor.shape
    panel_width = inverses.shape[1]
    z, xh, xl = lax.axis_index("z"), lax.axis_index("xh"), lax.axis_index("xl")
    y, core = lax.axis_index("y"), lax.axis_index("core")
    x = xh * 2 + xl
    spot = jnp.stack([z, xh, xl, y, core]).astype(jnp.int32)
    device = device_of(z, xh, xl, y, core)
    panel = factor[:, :panel_width]
    row = lax.broadcasted_iota(jnp.int32, panel.shape, 0) + device * part
    col = lax.broadcasted_iota(jnp.int32, panel.shape, 1)
    panel = panel + jnp.where(row == col, damping[:, None], 0.0)

    from_first = lambda zz, xx, yy, cc: zz == 0 and xx == 0
    from_second = lambda zz, xx, yy, cc: zz == 0 and xx == 1
    lead = [swap(panel, dx=2, only=from_first), swap(panel, dx=3, only=from_second), panel]
    pieces = spread_corner(panel, z, x, y)
    ends = jnp.where(y < 2, lead[2], lead[0])
    ends = jnp.concatenate([lead[1], ends], axis=0)
    lines = jnp.stack([ends] + [swap(ends, dy=m, only=on_line) for m in (1, 2, 3)])
    cols_share = share_cols(panel)
    rows_share = share_rows(panel)
    second = swap(factor[:, panel_width : 3 * panel_width], dx=3, only=from_second)
    cols_in = lax.all_gather(cols_share, ("z", "xh"), tiled=True)
    rows_in = lax.all_gather(rows_share, ("xl", "y", "core"), tiled=True)
    blocks = send_tiles(spot, factor, damping[None, :])

    lower = [
        lead[0],
        jnp.concatenate([lead[1], second], axis=1),
        factor[:, : 5 * panel_width],
    ]
    lines_other = swap(lines, dcore=1, only=on_line)
    lower_other = [swap(value, dcore=1, only=on_line) for value in lower]

    x_inverse, inverse = inverse_factor(spot, pieces)
    panels = place_panels(spot, lines, lines_other)
    row_factor, col_factor, tiles = panel_solve(spot, x_inverse, rows_in, cols_in)

    solved = forward_solve(spot, x_inverse, inverse, gradients, inverses, panels, lower, lower_other)
    solution_rows = spread_solution(spot, solved, z, x, y, core)

    out = update(blocks, row_factor, col_factor, None)
    out = update(blocks, row_factor, col_factor, out)
    tile = order // 64
    updated = out.reshape(8, 1, tile, 4, 1, tile)
    panel_tiles = tiles.reshape(8, 1, part // 8, panel_width)
    return (updated, panel_tiles, solution_rows)


def solution(mesh):
    split = Mesh(mesh.devices.reshape(4, 2, 2, 4, 2), ALL)
    row, col = ("z", "xh"), ("xl", "y", "core")
    return jax.shard_map(
        program,
        mesh=split,
        in_specs=(P(row + col, None), P(row + col), P(), P()),
        out_specs=(P(None, row, None, None, col, None), P(None, row, col, None), P()),
        check_vma=False,
    )
```

```python
import functools

import jax
import jax.numpy as jnp
from jax import lax
from jax.experimental import pallas as pl
from jax.experimental.pallas import tpu as pltpu
from jax.sharding import Mesh
from jax.sharding import PartitionSpec as P


INTERPRET = False
ALL = ("z", "xh", "xl", "y", "core")
VMEM = pl.BlockSpec(memory_space=pltpu.VMEM)
SMEM = pl.BlockSpec(memory_space=pltpu.SMEM)
ANY = pl.BlockSpec(memory_space=pl.ANY)
F32 = jnp.float32


def shape(*dims):
    return jax.ShapeDtypeStruct(dims, F32)


def dot(left, right, dims):
    return lax.dot_general(
        left, right, (dims, ((), ())), precision=lax.Precision.HIGHEST, preferred_element_type=F32
    )


def halves(value):
    high = value.astype(jnp.bfloat16)
    return high, (value - high.astype(F32)).astype(jnp.bfloat16)


def dot3(left, right, dims):
    one = lambda a, b: lax.dot_general(a, b, (dims, ((), ())), preferred_element_type=F32)
    return one(left[0], right[0]) + (one(left[0], right[1]) + one(left[1], right[0]))


NN = ((1,), (0,))
NT = ((1,), (1,))
TN = ((0,), (0,))


def device_of(z, xh, xl, y, core):
    return (((z * 2 + xh) * 2 + xl) * 4 + y) * 2 + core


def every():
    return [
        (z, xh, xl, y, core)
        for z in range(4)
        for xh in range(2)
        for xl in range(2)
        for y in range(4)
        for core in range(2)
    ]


def swap(value, dz=0, dx=0, dy=0, dcore=0, only=None):
    pairs = []
    for z, xh, xl, y, core in every():
        if only is None or only(z, xh * 2 + xl, y, core):
            to = (z ^ dz, xh ^ (dx >> 1), xl ^ (dx & 1), y ^ dy, core ^ dcore)
            pairs.append((device_of(z, xh, xl, y, core), device_of(*to)))
    return lax.ppermute(value, ALL, pairs)


def factor_block(block):
    size = block.shape[0]
    lane = lax.broadcasted_iota(jnp.int32, (8, size), 1)
    sub = lax.broadcasted_iota(jnp.int32, (8, size), 0)
    left = [block[8 * i : 8 * i + 8, :] for i in range(size // 8)]
    right = [jnp.where(lane == sub + 8 * i, 1.0, 0.0).astype(F32) for i in range(size // 8)]
    for k in range(size - 1):
        b, s = divmod(k, 8)
        inverse = 1.0 / left[b][s : s + 1, k : k + 1]
        left_row = jnp.broadcast_to(left[b][s : s + 1, :] * inverse, (8, size))
        right_row = jnp.broadcast_to(right[b][s : s + 1, :] * inverse, (8, size))
        for i in range(b if s < 7 else b + 1, size // 8):
            col = jnp.broadcast_to(left[i][:, k : k + 1], (8, size))
            if i == b:
                col = jnp.where(sub > s, col, 0.0)
            left[i] = left[i] - col * left_row
            right[i] = right[i] - col * right_row
    rows = []
    for i in range(size // 8):
        pivot = jnp.sum(jnp.where(lane == sub + 8 * i, left[i], 0.0), axis=1, keepdims=True)
        rows.append(right[i] * (1.0 / jnp.sqrt(pivot)))
    return jnp.concatenate(rows, axis=0)


def corner_kernel(spot_ref, *refs):
    pieces = refs[:4]
    x_ref, square_ref, w_ref = refs[-3:]
    n = x_ref.shape[0]
    nb = n // 4
    part = pieces[0].shape[1]
    z = spot_ref[0]
    core = spot_ref[4]
    for q in range(4):
        for i in range(4):
            side = core if i < 2 else 1 - core
            row = pl.multiple_of((i % 2) * (n // 2) + side * (n // 4) + (z ^ q) * part, part)
            w_ref[pl.ds(row, part), :] = pieces[q][i]
    ri = lax.broadcasted_iota(jnp.int32, (n, n), 0)
    ci = lax.broadcasted_iota(jnp.int32, (n, n), 1)
    x_ref[...] = jnp.where(ri == ci, 1.0, 0.0).astype(F32)

    def step(j, carry):
        at = pl.multiple_of(j * nb, nb)
        xj = factor_block(w_ref[pl.ds(at, nb), pl.ds(at, nb)])
        low = dot(w_ref[:, pl.ds(at, nb)], xj, NT)
        rows = lax.broadcasted_iota(jnp.int32, (n, nb), 0)
        low = jnp.where(rows >= at + nb, low, 0.0)
        w_ref[...] = w_ref[...] - dot(low, low, NT)
        xr = dot(xj, x_ref[pl.ds(at, nb), :], NN)
        x_ref[pl.ds(at, nb), :] = xr
        x_ref[...] = x_ref[...] - dot(low, xr, NN)
        return carry

    lax.fori_loop(0, 4, step, 0)
    x = x_ref[...]
    square_ref[...] = dot(x, x, TN)


def inverse_factor(spot, pieces):
    n = pieces[0].shape[2]
    return pl.pallas_call(
        corner_kernel,
        out_shape=[shape(n, n), shape(n, n)],
        in_specs=[SMEM] + [VMEM] * 4,
        out_specs=[VMEM, VMEM],
        scratch_shapes=[pltpu.VMEM((n, n), F32)],
        interpret=INTERPRET,
        name="inverse_factor",
    )(spot, *pieces)


def spread_corner(panel, z, x, y):
    part = panel.shape[0] // 4
    pieces = [panel[d * part : (d + 1) * part] for d in range(4)]
    source = lambda zz, xx, yy, cc: zz == 0 and xx == 0 and yy < 2
    got = [swap(pieces[d], dz=d, only=source) for d in (1, 2, 3)]
    value = jnp.where(z == 0, pieces[0], got[0] + got[1] + got[2])
    source = lambda zz, xx, yy, cc: xx == 0 and yy < 2
    got = [swap(value, dx=d, only=source) for d in (1, 2, 3)]
    value = jnp.where(x == 0, value, got[0] + got[1] + got[2])
    source = lambda zz, xx, yy, cc: yy < 2
    got = [swap(value, dy=d, only=source) for d in (1, 2, 3)]
    upper = jnp.where(y == 0, value, jnp.where(y == 1, got[0], jnp.where(y == 2, got[1], got[2])))
    lower = jnp.where(y == 1, value, jnp.where(y == 0, got[0], jnp.where(y == 3, got[1], got[2])))
    both = jnp.stack([upper, lower])
    value = jnp.concatenate([both, swap(both, dcore=1)], axis=0)
    return [value] + [swap(value, dz=d) for d in (1, 2, 3)]


def pack_kernel(spot_ref, factor_ref, damping_ref, out_ref, hold):
    rows = hold.shape[0]
    part = damping_ref.shape[1]
    count, _, cols = out_ref.shape
    width = cols // 4
    z, xh, xl, y, core = (spot_ref[i] for i in range(5))
    hold[...] = factor_ref[...]
    device = (((z * 2 + xh) * 2 + xl) * 4 + y) * 2 + core
    at = pl.multiple_of(device * part, part)
    lane = lax.broadcasted_iota(jnp.int32, (rows, part), 1)
    sub = lax.broadcasted_iota(jnp.int32, (rows, part), 0)
    damping = jnp.broadcast_to(damping_ref[...], (rows, part))
    add = jnp.where(lane == sub + pl.program_id(0) * rows, damping, 0.0)
    hold[:, pl.ds(at, part)] = hold[:, pl.ds(at, part)] + add
    for m in range(count):
        for b in range(4):
            col = b * count + m
            out_ref[m, :, b * width : (b + 1) * width] = hold[:, col * width : (col + 1) * width]


def send_tiles(spot, factor, damping):
    part, order = factor.shape
    rows = part // 4
    cols = order // 16
    packed = pl.pallas_call(
        pack_kernel,
        out_shape=shape(16, part, cols),
        grid=(4,),
        in_specs=[SMEM, pl.BlockSpec((rows, order), lambda i: (i, 0)), VMEM],
        out_specs=pl.BlockSpec((16, rows, cols), lambda i: (0, i, 0)),
        scratch_shapes=[pltpu.VMEM((rows, order), F32)],
        interpret=INTERPRET,
        name="pack_tiles",
    )(spot, factor, damping)
    packed = lax.all_to_all(packed, ("xl", "y", "core"), 0, 0, tiled=True)
    return lax.all_to_all(packed.reshape(8, 2 * part, cols), ("z", "xh"), 0, 0, tiled=True)


def panel_kernel(spot_ref, x_ref, rows_ref, cols_ref, row_ref, col_ref, tile_ref):
    part = rows_ref.shape[0] // 16
    xl, y, core = spot_ref[2], spot_ref[3], spot_ref[4]
    x = halves(x_ref[...])
    row_ref[...] = dot3(halves(rows_ref[...]), x, NT)
    col_ref[...] = dot3(halves(cols_ref[...]), x, NT)
    share = part // 8
    column = (xl * 4 + y) * 2 + core
    for a in range(8):
        at = pl.multiple_of(a * 2 * part + column * share, share)
        tile_ref[a * share : (a + 1) * share, :] = row_ref[pl.ds(at, share), :]


def panel_solve(spot, x, rows_in, cols_in):
    width = x.shape[0]
    return pl.pallas_call(
        panel_kernel,
        out_shape=[shape(*rows_in.shape), shape(*cols_in.shape), shape(rows_in.shape[0] // 16, width)],
        in_specs=[SMEM, VMEM, VMEM, VMEM],
        out_specs=[VMEM] * 3,
        interpret=INTERPRET,
        name="panel_solve",
    )(spot, x, rows_in, cols_in)


def share_rows(panel):
    pairs = []
    for z, xh, xl, y, core in every():
        to = (xl * 2 + (y >> 1), y & 1, z >> 1, (z & 1) * 2 + xh, core)
        pairs.append((device_of(z, xh, xl, y, core), device_of(*to)))
    return lax.ppermute(panel, ALL, pairs)


def share_cols(panel):
    pairs = []
    for z, xh, xl, y, core in every():
        to = (z, core, xh, xl * 2 + (y >> 1), y & 1)
        pairs.append((device_of(z, xh, xl, y, core), device_of(*to)))
    return lax.ppermute(panel, ALL, pairs)


def update_kernel(block_ref, row_ref, col_ref, *refs):
    out_ref, high_ref, low_ref, hold = refs[-4:]

    @pl.when(pl.program_id(0) == 0)
    def _():
        high_ref[...], low_ref[...] = halves(col_ref[...])

    left = halves(row_ref[...])
    hold[...] = block_ref[0] - dot3(left, (high_ref[...], low_ref[...]), NT)
    rows, cols = hold.shape
    lanes = out_ref.shape[1]
    groups = cols // lanes
    for g in range(groups):
        out_ref[pl.ds(g, rows, stride=groups), :] = hold[:, g * lanes : (g + 1) * lanes]


def update(blocks, row_factor, col_factor, out):
    count, rows, cols = blocks.shape
    half = count // 2
    first = 0 if out is None else half
    width = row_factor.shape[1]
    lanes = cols // 8
    return pl.pallas_call(
        update_kernel,
        out_shape=shape(count * rows * 8, lanes),
        grid=(half,),
        in_specs=[
            pl.BlockSpec((1, rows, cols), lambda i: (i + first, 0, 0)),
            pl.BlockSpec((rows, width), lambda i: (i + first, 0)),
            pl.BlockSpec(col_factor.shape, lambda i: (0, 0)),
        ]
        + ([] if out is None else [ANY]),
        out_specs=pl.BlockSpec((rows * 8, lanes), lambda i: (i + first, 0)),
        scratch_shapes=[
            pltpu.VMEM(col_factor.shape, jnp.bfloat16),
            pltpu.VMEM(col_factor.shape, jnp.bfloat16),
            pltpu.VMEM((rows, cols), F32),
        ],
        input_output_aliases={} if out is None else {3: 0},
        interpret=INTERPRET,
        name="update",
    )(blocks, row_factor, col_factor, *([] if out is None else [out]))


def on_line(z, x, y, core):
    return z == 0 and x == 2


def place_panels_kernel(spot_ref, own_ref, other_ref, tie_own_ref, tie_other_ref, out_ref, tie_ref):
    part = own_ref.shape[1] // 2
    y, core = spot_ref[3], spot_ref[4]
    for ref, side in ((own_ref, core), (other_ref, 1 - core)):
        for m in range(4):
            line = y ^ m
            for slot, tile in ((0, 4 + line), (1, line + 8 * (1 - line // 2))):
                at = (tile * 2 + side) * part
                out_ref[:, pl.ds(pl.multiple_of(at, part), part)] = ref[
                    m, slot * part : (slot + 1) * part, :
                ].T
    for ref, side in ((tie_own_ref, core), (tie_other_ref, 1 - core)):
        for c in range(2):
            at = pl.multiple_of((c * 2 + side) * part, part)
            for i in range(2):
                tie_ref[i, pl.ds(at, part), :] = ref[y ^ c, i * part : (i + 1) * part, :]


def place_panels(spot, own, other, tie_own, tie_other):
    _, rows, width = own.shape
    return pl.pallas_call(
        place_panels_kernel,
        out_shape=[shape(width, 12 * rows), shape(2, width, width)],
        in_specs=[SMEM] + [VMEM] * 4,
        out_specs=[VMEM, VMEM],
        interpret=INTERPRET,
        name="place_panels",
    )(spot, own, other, tie_own, tie_other)


def dot_e(left, right, dims):
    return dot3(halves(left), halves(right), dims)


def write_share(spot_ref, grads_ref, share_ref, sources, known, v, slots):
    y, core = spot_ref[3], spot_ref[4]
    panel = v.shape[0]
    part = panel // 4
    slot = jnp.where(y < 2, slots[0], slots[1])
    start = (slot * 4 + y) * 2 * part
    for refs, side in ((sources[0], core), (sources[1], 1 - core)):
        total = None
        for j, value in enumerate([v] + known):
            low, high = j * panel, (j + 1) * panel
            rows = refs[0][:, low:high]
            if len(refs) == 2:
                rows = jnp.where(y < 2, refs[1][:, low:high], rows)
            term = dot_e(rows, value, NN)
            total = term if total is None else total + term
        at = pl.multiple_of(side * part, part)
        row = pl.multiple_of(start + at, part)
        share_ref[pl.ds(at, part), :] = grads_ref[pl.ds(row, part), :] - total


def pick(shares, y, line):
    near = jnp.where(y == (line ^ 2), shares[2], shares[3])
    return jnp.where(y == line, shares[0], jnp.where(y == (line ^ 1), shares[1], near))


def right_sides(refs, y):
    shares = [ref[...] for ref in refs]
    odd = jnp.concatenate([pick(shares, y, 2), pick(shares, y, 3)], axis=0)
    return odd, shares


def solve_first_kernel(spot_ref, grads_ref, x_ref, square_ref, a0, b0, a1, b1, y_ref, v_ref, share_ref):
    panel = x_ref.shape[0]
    lead = grads_ref[0:panel, :]
    v = dot_e(square_ref[...], lead, NN)
    write_share(spot_ref, grads_ref, share_ref, ((a0, a1), (b0, b1)), [], v, (1, 0))
    y_ref[...] = dot_e(x_ref[...], lead, NN)
    v_ref[...] = v


def solve_pair_kernel(spot_ref, grads_ref, *refs, pair):
    shares, refs = refs[:4], list(refs[4:])
    inverse_a, inverse_b, square_ref, panel_a, panel_b, tie_ref, v_ref = refs[:7]
    known = [ref[...] for ref in refs[7 : 7 + 2 * pair]]
    refs = refs[7 + 2 * pair :]
    y_a_ref, y_b_ref, v_out, share_ref = refs[-4:]
    sources = refs[:-4]
    y = spot_ref[3]
    square = square_ref[...]
    right, values = right_sides(shares, y)
    y_a = dot_e(inverse_a[0], right, NN)
    move = dot_e(square, dot_e(panel_a[...], y_a, NN), NN)
    right = jnp.concatenate([pick(values, y, 0), pick(values, y, 1)], axis=0)
    right = right - dot_e(tie_ref[0], y_a, NN) + dot_e(panel_b[...], move, TN)
    y_b = dot_e(inverse_b[0], right, NN)
    v = v_ref[...] - move - dot_e(square, dot_e(panel_b[...], y_b, NN), NN)
    half = len(sources) // 2
    slots = (2, 1) if pair == 0 else (2, 2)
    write_share(spot_ref, grads_ref, share_ref, (sources[:half], sources[half:]), known + [y_a, y_b], v, slots)
    y_a_ref[...] = y_a
    y_b_ref[...] = y_b
    v_out[...] = v


def solve_last_kernel(spot_ref, *refs):
    right, _ = right_sides(refs[:4], spot_ref[3])
    refs[5][...] = dot_e(refs[4][0], right, NN)


def forward_solve(spot, x, square, grads, inverses, panels, ties, own, other):
    panel = x.shape[0]
    count = grads.shape[1]
    full, tile = shape(panel, count), shape(panel // 2, count)

    def run(kernel, operands, specs, outs):
        return pl.pallas_call(
            kernel,
            out_shape=outs,
            grid=(1,),
            in_specs=[SMEM] + specs,
            out_specs=[VMEM] * len(outs),
            interpret=INTERPRET,
            name="solve",
        )(spot, *operands)

    def exchange(share):
        return [share] + [swap(share, dy=m, only=on_line) for m in (1, 2, 3)]

    inverse = lambda b: pl.BlockSpec((1, panel, panel), lambda i: (b - 1, 0, 0))
    leading = lambda b: pl.BlockSpec((panel, panel), lambda i: (0, b))
    operands = [grads, x, square, own[0], other[0], own[1], other[1]]
    first, v, share = run(solve_first_kernel, operands, [VMEM] * 7, [full, full, tile])
    solved = [first]
    for pair in range(2):
        a, b = 2 * pair + 1, 2 * pair + 2
        operands = [grads, *exchange(share), inverses, inverses, square, panels, panels, ties, v]
        specs = [VMEM] * 5 + [inverse(a), inverse(b), VMEM, leading(a), leading(b)]
        specs += [pl.BlockSpec((1, panel, panel), lambda i, p=pair: (p, 0, 0)), VMEM]
        rest = solved[1:] + ([own[1], own[2], other[1], other[2]] if pair == 0 else [own[2], other[2]])
        outs = [full, full, full, tile]
        kernel = functools.partial(solve_pair_kernel, pair=pair)
        y_a, y_b, v, share = run(kernel, operands + rest, specs + [VMEM] * len(rest), outs)
        solved += [y_a, y_b]
    operands = [*exchange(share), inverses]
    solved += run(solve_last_kernel, operands, [VMEM] * 4 + [inverse(5)], [full])
    return solved


def spread_solution(spot, solved, z, x, y, core):
    whole = jnp.concatenate(solved, axis=0)
    rows = whole.shape[0]
    own = lax.dynamic_slice_in_dim(whole, (y * 2 + core) * (rows // 8), rows // 8, 0)
    got = [swap(own, dx=d, only=on_line) for d in (1, 2, 3)]
    own = jnp.where(x == 2, own, got[0] + got[1] + got[2])
    source = lambda zz, xx, yy, cc: zz == 0
    got = [swap(own, dz=d, only=source) for d in (1, 2, 3)]
    own = jnp.where(z == 0, own, got[0] + got[1] + got[2])
    lines = jnp.stack([own] + [swap(own, dy=d) for d in (1, 2, 3)])
    other = swap(lines, dcore=1)
    return pl.pallas_call(
        place_rows_kernel,
        out_shape=shape(*whole.shape),
        in_specs=[SMEM, VMEM, VMEM],
        out_specs=VMEM,
        interpret=INTERPRET,
        name="place_rows",
    )(spot, lines, other)


def place_rows_kernel(spot_ref, own_ref, other_ref, out_ref):
    rows = own_ref.shape[1]
    y, core = spot_ref[3], spot_ref[4]
    for ref, side in ((own_ref, core), (other_ref, 1 - core)):
        for m in range(4):
            at = ((y ^ m) * 2 + side) * rows
            out_ref[pl.ds(pl.multiple_of(at, rows), rows), :] = ref[m]


def program(factor, damping, gradients, inverses):
    part, order = factor.shape
    panel_width = inverses.shape[1]
    z, xh, xl = lax.axis_index("z"), lax.axis_index("xh"), lax.axis_index("xl")
    y, core = lax.axis_index("y"), lax.axis_index("core")
    x = xh * 2 + xl
    spot = jnp.stack([z, xh, xl, y, core]).astype(jnp.int32)
    device = device_of(z, xh, xl, y, core)
    panel = factor[:, :panel_width]
    row = lax.broadcasted_iota(jnp.int32, panel.shape, 0) + device * part
    col = lax.broadcasted_iota(jnp.int32, panel.shape, 1)
    panel = panel + jnp.where(row == col, damping[:, None], 0.0)

    from_first = lambda zz, xx, yy, cc: zz == 0 and xx == 0
    from_second = lambda zz, xx, yy, cc: zz == 0 and xx == 1
    moved = swap(factor[:, : 2 * panel_width], dx=3, only=from_second)
    lead = [swap(panel, dx=2, only=from_first), moved[:, :panel_width], panel]
    pieces = spread_corner(panel, z, x, y)
    ends = jnp.where(y < 2, lead[2], lead[0])
    ends = jnp.concatenate([lead[1], ends], axis=0)
    lines = jnp.stack([ends] + [swap(ends, dy=m, only=on_line) for m in (1, 2, 3)])
    tie = factor[:, 3 * panel_width : 4 * panel_width]
    tie = jnp.concatenate([moved[:, panel_width:], tie], axis=0)
    from_low = lambda zz, xx, yy, cc: on_line(zz, xx, yy, cc) and yy < 2
    ties = jnp.stack([tie] + [swap(tie, dy=m, only=from_low) for m in (1, 2, 3)])
    cols_share = share_cols(panel)
    rows_share = share_rows(panel)
    second = swap(factor[:, 2 * panel_width : 3 * panel_width], dx=3, only=from_second)
    cols_in = lax.all_gather(cols_share, ("z", "xh"), tiled=True)
    rows_in = lax.all_gather(rows_share, ("xl", "y", "core"), tiled=True)
    blocks = send_tiles(spot, factor, damping[None, :])

    lower = [
        lead[0],
        jnp.concatenate([moved, second], axis=1),
        factor[:, : 5 * panel_width],
    ]
    lines_other = swap(lines, dcore=1, only=on_line)
    ties_other = swap(ties, dcore=1, only=on_line)
    lower_other = [swap(value, dcore=1, only=on_line) for value in lower]

    x_inverse, inverse = inverse_factor(spot, pieces)
    panels, ties = place_panels(spot, lines, lines_other, ties, ties_other)
    row_factor, col_factor, tiles = panel_solve(spot, x_inverse, rows_in, cols_in)

    solved = forward_solve(spot, x_inverse, inverse, gradients, inverses, panels, ties, lower, lower_other)
    solution_rows = spread_solution(spot, solved, z, x, y, core)

    out = update(blocks, row_factor, col_factor, None)
    out = update(blocks, row_factor, col_factor, out)
    tile = order // 64
    updated = out.reshape(8, 1, tile, 4, 1, tile)
    panel_tiles = tiles.reshape(8, 1, part // 8, panel_width)
    return (updated, panel_tiles, solution_rows)


def solution(mesh):
    split = Mesh(mesh.devices.reshape(4, 2, 2, 4, 2), ALL)
    row, col = ("z", "xh"), ("xl", "y", "core")
    return jax.shard_map(
        program,
        mesh=split,
        in_specs=(P(row + col, None), P(row + col), P(), P()),
        out_specs=(P(None, row, None, None, col, None), P(None, row, col, None), P()),
        check_vma=False,
    )
```

```python
import functools

import jax
import jax.numpy as jnp
from jax import lax
from jax.experimental import pallas as pl
from jax.experimental.pallas import tpu as pltpu
from jax.sharding import Mesh
from jax.sharding import PartitionSpec as P


INTERPRET = False
ALL = ("z", "xh", "xl", "y", "core")
VMEM = pl.BlockSpec(memory_space=pltpu.VMEM)
SMEM = pl.BlockSpec(memory_space=pltpu.SMEM)
ANY = pl.BlockSpec(memory_space=pl.ANY)
F32 = jnp.float32


def shape(*dims):
    return jax.ShapeDtypeStruct(dims, F32)


def dot(left, right, dims):
    return lax.dot_general(
        left, right, (dims, ((), ())), precision=lax.Precision.HIGHEST, preferred_element_type=F32
    )


def halves(value):
    high = value.astype(jnp.bfloat16)
    return high, (value - high.astype(F32)).astype(jnp.bfloat16)


def dot3(left, right, dims):
    one = lambda a, b: lax.dot_general(a, b, (dims, ((), ())), preferred_element_type=F32)
    return one(left[0], right[0]) + (one(left[0], right[1]) + one(left[1], right[0]))


NN = ((1,), (0,))
NT = ((1,), (1,))
TN = ((0,), (0,))


def device_of(z, xh, xl, y, core):
    return (((z * 2 + xh) * 2 + xl) * 4 + y) * 2 + core


def every():
    return [
        (z, xh, xl, y, core)
        for z in range(4)
        for xh in range(2)
        for xl in range(2)
        for y in range(4)
        for core in range(2)
    ]


def swap(value, dz=0, dx=0, dy=0, dcore=0, only=None):
    pairs = []
    for z, xh, xl, y, core in every():
        if only is None or only(z, xh * 2 + xl, y, core):
            to = (z ^ dz, xh ^ (dx >> 1), xl ^ (dx & 1), y ^ dy, core ^ dcore)
            pairs.append((device_of(z, xh, xl, y, core), device_of(*to)))
    return lax.ppermute(value, ALL, pairs)


def factor_block(block):
    size = block.shape[0]
    lane = lax.broadcasted_iota(jnp.int32, (8, size), 1)
    sub = lax.broadcasted_iota(jnp.int32, (8, size), 0)
    left = [block[8 * i : 8 * i + 8, :] for i in range(size // 8)]
    right = [jnp.where(lane == sub + 8 * i, 1.0, 0.0).astype(F32) for i in range(size // 8)]
    for k in range(size - 1):
        b, s = divmod(k, 8)
        inverse = 1.0 / left[b][s : s + 1, k : k + 1]
        left_row = jnp.broadcast_to(left[b][s : s + 1, :] * inverse, (8, size))
        right_row = jnp.broadcast_to(right[b][s : s + 1, :] * inverse, (8, size))
        for i in range(b if s < 7 else b + 1, size // 8):
            col = jnp.broadcast_to(left[i][:, k : k + 1], (8, size))
            if i == b:
                col = jnp.where(sub > s, col, 0.0)
            left[i] = left[i] - col * left_row
            right[i] = right[i] - col * right_row
    rows = []
    for i in range(size // 8):
        pivot = jnp.sum(jnp.where(lane == sub + 8 * i, left[i], 0.0), axis=1, keepdims=True)
        rows.append(right[i] * (1.0 / jnp.sqrt(pivot)))
    return jnp.concatenate(rows, axis=0)


def corner_kernel(spot_ref, *refs):
    pieces = refs[:4]
    x_ref, square_ref, w_ref = refs[-3:]
    n = x_ref.shape[0]
    nb = n // 4
    part = pieces[0].shape[1]
    z = spot_ref[0]
    core = spot_ref[4]
    for q in range(4):
        for i in range(4):
            side = core if i < 2 else 1 - core
            row = pl.multiple_of((i % 2) * (n // 2) + side * (n // 4) + (z ^ q) * part, part)
            w_ref[pl.ds(row, part), :] = pieces[q][i]
    ri = lax.broadcasted_iota(jnp.int32, (n, n), 0)
    ci = lax.broadcasted_iota(jnp.int32, (n, n), 1)
    x_ref[...] = jnp.where(ri == ci, 1.0, 0.0).astype(F32)

    def step(j, carry):
        at = pl.multiple_of(j * nb, nb)
        xj = factor_block(w_ref[pl.ds(at, nb), pl.ds(at, nb)])
        low = dot(w_ref[:, pl.ds(at, nb)], xj, NT)
        rows = lax.broadcasted_iota(jnp.int32, (n, nb), 0)
        low = jnp.where(rows >= at + nb, low, 0.0)
        w_ref[...] = w_ref[...] - dot(low, low, NT)
        xr = dot(xj, x_ref[pl.ds(at, nb), :], NN)
        x_ref[pl.ds(at, nb), :] = xr
        x_ref[...] = x_ref[...] - dot(low, xr, NN)
        return carry

    lax.fori_loop(0, 4, step, 0)
    x = x_ref[...]
    square_ref[...] = dot(x, x, TN)


def inverse_factor(spot, pieces):
    n = pieces[0].shape[2]
    return pl.pallas_call(
        corner_kernel,
        out_shape=[shape(n, n), shape(n, n)],
        in_specs=[SMEM] + [VMEM] * 4,
        out_specs=[VMEM, VMEM],
        scratch_shapes=[pltpu.VMEM((n, n), F32)],
        interpret=INTERPRET,
        name="inverse_factor",
    )(spot, *pieces)


def spread_corner(panel, z, x, y):
    part = panel.shape[0] // 4
    pieces = [panel[d * part : (d + 1) * part] for d in range(4)]
    source = lambda zz, xx, yy, cc: zz == 0 and xx == 0 and yy < 2
    got = [swap(pieces[d], dz=d, only=source) for d in (1, 2, 3)]
    value = jnp.where(z == 0, pieces[0], got[0] + got[1] + got[2])
    source = lambda zz, xx, yy, cc: xx == 0 and yy < 2
    got = [swap(value, dx=d, only=source) for d in (1, 2, 3)]
    value = jnp.where(x == 0, value, got[0] + got[1] + got[2])
    source = lambda zz, xx, yy, cc: yy < 2
    got = [swap(value, dy=d, only=source) for d in (1, 2, 3)]
    upper = jnp.where(y == 0, value, jnp.where(y == 1, got[0], jnp.where(y == 2, got[1], got[2])))
    lower = jnp.where(y == 1, value, jnp.where(y == 0, got[0], jnp.where(y == 3, got[1], got[2])))
    both = jnp.stack([upper, lower])
    value = jnp.concatenate([both, swap(both, dcore=1)], axis=0)
    return [value] + [swap(value, dz=d) for d in (1, 2, 3)]


def pack_kernel(spot_ref, factor_ref, damping_ref, out_ref, hold):
    rows = hold.shape[0]
    part = damping_ref.shape[1]
    count, _, cols = out_ref.shape
    width = cols // 4
    z, xh, xl, y, core = (spot_ref[i] for i in range(5))
    hold[...] = factor_ref[...]
    device = (((z * 2 + xh) * 2 + xl) * 4 + y) * 2 + core
    at = pl.multiple_of(device * part, part)
    lane = lax.broadcasted_iota(jnp.int32, (rows, part), 1)
    sub = lax.broadcasted_iota(jnp.int32, (rows, part), 0)
    damping = jnp.broadcast_to(damping_ref[...], (rows, part))
    add = jnp.where(lane == sub + pl.program_id(0) * rows, damping, 0.0)
    hold[:, pl.ds(at, part)] = hold[:, pl.ds(at, part)] + add
    for m in range(count):
        for b in range(4):
            col = b * count + m
            out_ref[m, :, b * width : (b + 1) * width] = hold[:, col * width : (col + 1) * width]


def send_tiles(spot, factor, damping):
    part, order = factor.shape
    rows = part // 4
    cols = order // 16
    pack = pl.pallas_call(
        pack_kernel,
        out_shape=shape(16, part, cols),
        grid=(4,),
        in_specs=[SMEM, pl.BlockSpec((rows, order), lambda i: (i, 0)), VMEM],
        out_specs=pl.BlockSpec((16, rows, cols), lambda i: (0, i, 0)),
        scratch_shapes=[pltpu.VMEM((rows, order), F32)],
        interpret=INTERPRET,
        name="pack_tiles",
    )
    packed = pack(spot, factor, damping)
    packed = lax.all_to_all(packed, ("xl", "y", "core"), 0, 0, tiled=True)
    return lax.all_to_all(packed.reshape(8, 2 * part, cols), ("z", "xh"), 0, 0, tiled=True)


def panel_kernel(spot_ref, x_ref, rows_ref, cols_ref, row_ref, col_ref, tile_ref):
    part = rows_ref.shape[0] // 16
    xl, y, core = spot_ref[2], spot_ref[3], spot_ref[4]
    x = halves(x_ref[...])
    row_ref[...] = dot3(halves(rows_ref[...]), x, NT)
    col_ref[...] = dot3(halves(cols_ref[...]), x, NT)
    share = part // 8
    column = (xl * 4 + y) * 2 + core
    for a in range(8):
        at = pl.multiple_of(a * 2 * part + column * share, share)
        tile_ref[a * share : (a + 1) * share, :] = row_ref[pl.ds(at, share), :]


def panel_solve(spot, x, rows_in, cols_in):
    width = x.shape[0]
    return pl.pallas_call(
        panel_kernel,
        out_shape=[shape(*rows_in.shape), shape(*cols_in.shape), shape(rows_in.shape[0] // 16, width)],
        in_specs=[SMEM, VMEM, VMEM, VMEM],
        out_specs=[VMEM] * 3,
        interpret=INTERPRET,
        name="panel_solve",
    )(spot, x, rows_in, cols_in)


def share_rows(panel):
    pairs = []
    for z, xh, xl, y, core in every():
        to = (xl * 2 + (y >> 1), y & 1, z >> 1, (z & 1) * 2 + xh, core)
        pairs.append((device_of(z, xh, xl, y, core), device_of(*to)))
    return lax.ppermute(panel, ALL, pairs)


def share_cols(panel):
    pairs = []
    for z, xh, xl, y, core in every():
        to = (z, core, xh, xl * 2 + (y >> 1), y & 1)
        pairs.append((device_of(z, xh, xl, y, core), device_of(*to)))
    return lax.ppermute(panel, ALL, pairs)


def update_kernel(block_ref, row_ref, col_ref, *refs):
    out_ref, high_ref, low_ref, hold = refs[-4:]

    @pl.when(pl.program_id(0) == 0)
    def _():
        high_ref[...], low_ref[...] = halves(col_ref[...])

    left = halves(row_ref[...])
    hold[...] = block_ref[0] - dot3(left, (high_ref[...], low_ref[...]), NT)
    rows, cols = hold.shape
    lanes = out_ref.shape[1]
    groups = cols // lanes
    for g in range(groups):
        out_ref[pl.ds(g, rows, stride=groups), :] = hold[:, g * lanes : (g + 1) * lanes]


def update(blocks, row_factor, col_factor, out):
    count, rows, cols = blocks.shape
    half = count // 2
    first = 0 if out is None else half
    width = row_factor.shape[1]
    lanes = cols // 8
    return pl.pallas_call(
        update_kernel,
        out_shape=shape(count * rows * 8, lanes),
        grid=(half,),
        in_specs=[
            pl.BlockSpec((1, rows, cols), lambda i: (i + first, 0, 0)),
            pl.BlockSpec((rows, width), lambda i: (i + first, 0)),
            pl.BlockSpec(col_factor.shape, lambda i: (0, 0)),
        ]
        + ([] if out is None else [ANY]),
        out_specs=pl.BlockSpec((rows * 8, lanes), lambda i: (i + first, 0)),
        scratch_shapes=[
            pltpu.VMEM(col_factor.shape, jnp.bfloat16),
            pltpu.VMEM(col_factor.shape, jnp.bfloat16),
            pltpu.VMEM((rows, cols), F32),
        ],
        input_output_aliases={} if out is None else {3: 0},
        interpret=INTERPRET,
        name="update",
    )(blocks, row_factor, col_factor, *([] if out is None else [out]))


def on_line(z, x, y, core):
    return z == 0 and x == 2


def place_panels_kernel(spot_ref, own_ref, other_ref, tie_own_ref, tie_other_ref, out_ref, tie_ref):
    part = own_ref.shape[1] // 2
    y, core = spot_ref[3], spot_ref[4]
    for ref, side in ((own_ref, core), (other_ref, 1 - core)):
        for m in range(4):
            line = y ^ m
            for slot, tile in ((0, 4 + line), (1, line + 8 * (1 - line // 2))):
                at = (tile * 2 + side) * part
                out_ref[:, pl.ds(pl.multiple_of(at, part), part)] = ref[
                    m, slot * part : (slot + 1) * part, :
                ].T
    for ref, side in ((tie_own_ref, core), (tie_other_ref, 1 - core)):
        for c in range(2):
            at = pl.multiple_of((c * 2 + side) * part, part)
            for i in range(2):
                tie_ref[i, pl.ds(at, part), :] = ref[y ^ c, i * part : (i + 1) * part, :]


def place_panels(spot, own, other, tie_own, tie_other):
    _, rows, width = own.shape
    return pl.pallas_call(
        place_panels_kernel,
        out_shape=[shape(width, 12 * rows), shape(2, width, width)],
        in_specs=[SMEM] + [VMEM] * 4,
        out_specs=[VMEM, VMEM],
        interpret=INTERPRET,
        name="place_panels",
    )(spot, own, other, tie_own, tie_other)


def dot_e(left, right, dims):
    return dot3(halves(left), halves(right), dims)


def write_share(spot_ref, grads_ref, share_ref, sources, known, v, slots):
    y, core = spot_ref[3], spot_ref[4]
    panel = v.shape[0]
    part = panel // 4
    slot = jnp.where(y < 2, slots[0], slots[1])
    start = (slot * 4 + y) * 2 * part
    for refs, side in ((sources[0], core), (sources[1], 1 - core)):
        total = None
        for j, value in enumerate([v] + known):
            low, high = j * panel, (j + 1) * panel
            rows = refs[0][:, low:high]
            if len(refs) == 2:
                rows = jnp.where(y < 2, refs[1][:, low:high], rows)
            term = dot_e(rows, value, NN)
            total = term if total is None else total + term
        at = pl.multiple_of(side * part, part)
        row = pl.multiple_of(start + at, part)
        share_ref[pl.ds(at, part), :] = grads_ref[pl.ds(row, part), :] - total


def pick(shares, y, line):
    near = jnp.where(y == (line ^ 2), shares[2], shares[3])
    return jnp.where(y == line, shares[0], jnp.where(y == (line ^ 1), shares[1], near))


def right_sides(refs, y):
    shares = [ref[...] for ref in refs]
    odd = jnp.concatenate([pick(shares, y, 2), pick(shares, y, 3)], axis=0)
    return odd, shares


def solve_first_kernel(spot_ref, grads_ref, x_ref, square_ref, own_ref, other_ref, y_ref, v_ref, share_ref):
    panel = x_ref.shape[0]
    part = panel // 4
    sources = [(ref[0:part, :], ref[part : 2 * part, :]) for ref in (own_ref, other_ref)]
    lead = grads_ref[0:panel, :]
    v = dot_e(square_ref[...], lead, NN)
    write_share(spot_ref, grads_ref, share_ref, sources, [], v, (1, 0))
    y_ref[...] = dot_e(x_ref[...], lead, NN)
    v_ref[...] = v


def solve_pair_kernel(spot_ref, grads_ref, *refs, pair):
    shares, refs = refs[:4], list(refs[4:])
    inverse_a, inverse_b, square_ref, panel_a, panel_b, tie_ref, v_ref = refs[:7]
    known = [ref[...] for ref in refs[7 : 7 + 2 * pair]]
    refs = refs[7 + 2 * pair :]
    y_a_ref, y_b_ref, v_out, share_ref = refs[-4:]
    sources = refs[:-4]
    y = spot_ref[3]
    square = square_ref[...]
    right, values = right_sides(shares, y)
    y_a = dot_e(inverse_a[0], right, NN)
    move = dot_e(square, dot_e(panel_a[...], y_a, NN), NN)
    right = jnp.concatenate([pick(values, y, 0), pick(values, y, 1)], axis=0)
    right = right - dot_e(tie_ref[0], y_a, NN) + dot_e(panel_b[...], move, TN)
    y_b = dot_e(inverse_b[0], right, NN)
    v = v_ref[...] - move - dot_e(square, dot_e(panel_b[...], y_b, NN), NN)
    half = len(sources) // 2
    slots = (2, 1) if pair == 0 else (2, 2)
    write_share(spot_ref, grads_ref, share_ref, (sources[:half], sources[half:]), known + [y_a, y_b], v, slots)
    y_a_ref[...] = y_a
    y_b_ref[...] = y_b
    v_out[...] = v


def solve_last_kernel(spot_ref, *refs):
    right, _ = right_sides(refs[:4], spot_ref[3])
    refs[5][...] = dot_e(refs[4][0], right, NN)


def forward_solve(spot, x, square, grads, inverses, panels, ties, start, own, other):
    panel = x.shape[0]
    count = grads.shape[1]
    full, tile = shape(panel, count), shape(panel // 2, count)

    def run(kernel, operands, specs, outs):
        return pl.pallas_call(
            kernel,
            out_shape=outs,
            grid=(1,),
            in_specs=[SMEM] + specs,
            out_specs=[VMEM] * len(outs),
            interpret=INTERPRET,
            name="solve",
        )(spot, *operands)

    def exchange(share):
        return [share] + [swap(share, dy=m, only=on_line) for m in (1, 2, 3)]

    inverse = lambda b: pl.BlockSpec((1, panel, panel), lambda i: (b - 1, 0, 0))
    leading = lambda b: pl.BlockSpec((panel, panel), lambda i: (0, b))
    operands = [grads, x, square, *start]
    first, v, share = run(solve_first_kernel, operands, [VMEM] * 5, [full, full, tile])
    solved = [first]
    for pair in range(2):
        a, b = 2 * pair + 1, 2 * pair + 2
        operands = [grads, *exchange(share), inverses, inverses, square, panels, panels, ties, v]
        specs = [VMEM] * 5 + [inverse(a), inverse(b), VMEM, leading(a), leading(b)]
        specs += [pl.BlockSpec((1, panel, panel), lambda i, p=pair: (p, 0, 0)), VMEM]
        rest = solved[1:] + ([own[0], own[1], other[0], other[1]] if pair == 0 else [own[1], other[1]])
        outs = [full, full, full, tile]
        kernel = functools.partial(solve_pair_kernel, pair=pair)
        y_a, y_b, v, share = run(kernel, operands + rest, specs + [VMEM] * len(rest), outs)
        solved += [y_a, y_b]
    operands = [*exchange(share), inverses]
    solved += run(solve_last_kernel, operands, [VMEM] * 4 + [inverse(5)], [full])
    return solved


def spread_solution(spot, solved, z, x, y, core):
    whole = jnp.concatenate(solved, axis=0)
    rows = whole.shape[0]
    own = lax.dynamic_slice_in_dim(whole, (y * 2 + core) * (rows // 8), rows // 8, 0)
    got = [swap(own, dx=d, only=on_line) for d in (1, 2, 3)]
    own = jnp.where(x == 2, own, got[0] + got[1] + got[2])
    source = lambda zz, xx, yy, cc: zz == 0
    got = [swap(own, dz=d, only=source) for d in (1, 2, 3)]
    own = jnp.where(z == 0, own, got[0] + got[1] + got[2])
    lines = jnp.stack([own] + [swap(own, dy=d) for d in (1, 2, 3)])
    other = swap(lines, dcore=1)
    return pl.pallas_call(
        place_rows_kernel,
        out_shape=shape(*whole.shape),
        in_specs=[SMEM, VMEM, VMEM],
        out_specs=VMEM,
        interpret=INTERPRET,
        name="place_rows",
    )(spot, lines, other)


def place_rows_kernel(spot_ref, own_ref, other_ref, out_ref):
    rows = own_ref.shape[1]
    y, core = spot_ref[3], spot_ref[4]
    for ref, side in ((own_ref, core), (other_ref, 1 - core)):
        for m in range(4):
            at = ((y ^ m) * 2 + side) * rows
            out_ref[pl.ds(pl.multiple_of(at, rows), rows), :] = ref[m]


def program(factor, damping, gradients, inverses):
    part, order = factor.shape
    panel_width = inverses.shape[1]
    z, xh, xl = lax.axis_index("z"), lax.axis_index("xh"), lax.axis_index("xl")
    y, core = lax.axis_index("y"), lax.axis_index("core")
    x = xh * 2 + xl
    spot = jnp.stack([z, xh, xl, y, core]).astype(jnp.int32)
    device = device_of(z, xh, xl, y, core)
    panel = factor[:, :panel_width]
    row = lax.broadcasted_iota(jnp.int32, panel.shape, 0) + device * part
    col = lax.broadcasted_iota(jnp.int32, panel.shape, 1)
    panel = panel + jnp.where(row == col, damping[:, None], 0.0)

    from_first = lambda zz, xx, yy, cc: zz == 0 and xx == 0
    from_second = lambda zz, xx, yy, cc: zz == 0 and xx == 1
    moved = swap(factor[:, : 2 * panel_width], dx=3, only=from_second)
    lead = [swap(panel, dx=2, only=from_first), moved[:, :panel_width], panel]
    pieces = spread_corner(panel, z, x, y)
    ends = jnp.where(y < 2, lead[2], lead[0])
    ends = jnp.concatenate([lead[1], ends], axis=0)
    lines = jnp.stack([ends] + [swap(ends, dy=m, only=on_line) for m in (1, 2, 3)])
    tie = factor[:, 3 * panel_width : 4 * panel_width]
    tie = jnp.concatenate([moved[:, panel_width:], tie], axis=0)
    from_low = lambda zz, xx, yy, cc: on_line(zz, xx, yy, cc) and yy < 2
    ties = jnp.stack([tie] + [swap(tie, dy=m, only=from_low) for m in (1, 2, 3)])
    start_own = jnp.concatenate(lead[:2], axis=0)
    start_other = swap(start_own, dcore=1, only=on_line)
    cols_share = share_cols(panel)
    rows_share = share_rows(panel)
    second = swap(factor[:, 2 * panel_width : 3 * panel_width], dx=3, only=from_second)
    cols_in = lax.all_gather(cols_share, ("z", "xh"), tiled=True)
    rows_in = lax.all_gather(rows_share, ("xl", "y", "core"), tiled=True)
    blocks = send_tiles(spot, factor, damping[None, :])

    lower = [
        None,
        jnp.concatenate([moved, second], axis=1),
        factor[:, : 5 * panel_width],
    ]
    lines_other = swap(lines, dcore=1, only=on_line)
    ties_other = swap(ties, dcore=1, only=on_line)
    lower_other = [swap(value, dcore=1, only=on_line) for value in lower[1:]]

    x_inverse, inverse = inverse_factor(spot, pieces)
    panels, ties = place_panels(spot, lines, lines_other, ties, ties_other)
    row_factor, col_factor, tiles = panel_solve(spot, x_inverse, rows_in, cols_in)

    start = (start_own, start_other)
    solved = forward_solve(spot, x_inverse, inverse, gradients, inverses, panels, ties, start, lower[1:], lower_other)
    solution_rows = spread_solution(spot, solved, z, x, y, core)

    out = update(blocks, row_factor, col_factor, None)
    out = update(blocks, row_factor, col_factor, out)
    tile = order // 64
    updated = out.reshape(8, 1, tile, 4, 1, tile)
    panel_tiles = tiles.reshape(8, 1, part // 8, panel_width)
    return (updated, panel_tiles, solution_rows)


def solution(mesh):
    split = Mesh(mesh.devices.reshape(4, 2, 2, 4, 2), ALL)
    row, col = ("z", "xh"), ("xl", "y", "core")
    return jax.shard_map(
        program,
        mesh=split,
        in_specs=(P(row + col, None), P(row + col), P(), P()),
        out_specs=(P(None, row, None, None, col, None), P(None, row, col, None), P()),
        check_vma=False,
    )
```
